128 devices in a mesh: ctx: 64 (over z, y, x_lo, core), tp: 2 (over x_hi).
Axes of the slice: x: 4 (x_hi: 2, x_lo: 2; x = x_hi * 2 + x_lo), y: 4, z: 4, core: 2. Of those that a mesh axis runs over, the one named last changes fastest.
Arguments:
- queries: bfloat16 [32768, 4096], P('ctx', 'tp'), may hold values from -0.19921875 to 0.19921875
- keys: bfloat16 [32768, 4096], P('ctx', 'tp'), may hold values from -0.19921875 to 0.19921875
- values: bfloat16 [32768, 4096], P('ctx', 'tp'), may hold values from -0.19921875 to 0.19921875
- cotangent: bfloat16 [32768, 2048], P('ctx', 'tp'), may hold values from -6 to 6
- out_weight: bfloat16 [4096, 2048], P('tp'), may hold values from -0.125 to 0.125
- memory: float32 [32, 128, 128], P('tp'), may hold values from -0.6 to 0.6
Outputs:
- query_grad: bfloat16 [32768, 4096], P('ctx', 'tp')
- key_grad: bfloat16 [32768, 4096], P('ctx', 'tp')
- value_grad: bfloat16 [32768, 4096], P('ctx', 'tp')
- weight_grad: float32 [4096, 2048], P(('tp', 'ctx'))
The draws below stay inside these ranges and needn't reach their ends.
All inputs are finite; a program needn't handle non-finite values.
Results may differ from the reference program's by a relative error of at most 0.0058.
Values may be sent and summed in bfloat16 or wider, within the bound.
A program may use at most 320 MiB of HBM per device.

```python
import jax
import jax.numpy as jnp
from jax import lax

D = 2048
H = 32
E = 128
HD = 4096
TOK_DEV = 512
TOKENS = 32768


def levels(own_key, shape, pieces, least, top_value):
    loudness = 1.0
    for dim, shards_of in pieces:
        draws = jax.random.uniform(jax.random.fold_in(jax.random.fold_in(own_key, 6), dim), (shards_of,), jnp.float32, least / len(pieces), top_value / len(pieces))
        loudness = loudness * jnp.repeat(jnp.exp(draws), shape[dim] // shards_of).reshape((-1,) + (1,) * (len(shape) - 1 - dim))
    return loudness


def bell_draw(rng, dims, width, most, shards=(), kind=jnp.bfloat16):
    loudness = levels(rng, dims, shards, -0.22, 0.18) if shards else 1.0
    values = jax.random.normal(rng, dims, jnp.float32) * width * loudness
    return jnp.minimum(jnp.maximum(values, -most), most).astype(kind)


def setup_inputs(seed: int = 0) -> dict:
    splits = jax.random.split(jax.random.key(seed), 7)
    return {
        "queries": bell_draw(splits[0], (TOKENS, HD), 0.03, 0.19921875, ((0, 64), (1, 2))),
        "keys": bell_draw(splits[1], (TOKENS, HD), 0.03, 0.19921875, ((0, 64), (1, 2))),
        "values": bell_draw(splits[2], (TOKENS, HD), 0.03, 0.19921875, ((0, 64), (1, 2))),
        "cotangent": bell_draw(splits[3], (TOKENS, D), 1.0, 6.0, ((0, 64), (1, 2))),
        "out_weight": bell_draw(splits[4], (HD, D), D ** -0.5, 0.125, ((0, 2),)),
        "memory": bell_draw(splits[5], (H, E, E), 0.1, 0.6, ((0, 2),), jnp.float32),
    }


def reference(queries, keys, values, cotangent, out_weight, memory):
    tok_all, col_width = queries.shape
    heads = memory.shape[0]
    head_size = memory.shape[1]
    blocks = tok_all // TOK_DEV
    out_grad = jnp.dot(cotangent, out_weight.T, preferred_element_type=jnp.float32).astype(jnp.bfloat16)

    def split(array):
        return array.reshape(blocks, TOK_DEV, heads, head_size)

    query_b, key_b, value_b, grad_b = split(queries), split(keys), split(values), split(out_grad)
    kv_sum = jnp.einsum('cthe,cthf->chef', key_b.astype(jnp.float32), value_b.astype(jnp.float32))
    qd_sum = jnp.einsum('cthe,cthf->chef', query_b.astype(jnp.float32), grad_b.astype(jnp.float32))
    empty = jnp.zeros((1, heads, head_size, head_size), jnp.float32)
    before = jnp.concatenate([empty, jnp.cumsum(kv_sum, 0)[:-1]], 0)
    after = jnp.concatenate([jnp.cumsum(qd_sum[::-1], 0)[::-1][1:], empty], 0)
    state = (memory[None] + before).astype(jnp.bfloat16)
    adjoint = after.astype(jnp.bfloat16)
    causal = jnp.arange(TOK_DEV)[:, None] >= jnp.arange(TOK_DEV)[None, :]

    def one_block(parts):
        query, key, value, grad, state_c, adjoint_c = [p.astype(jnp.float32) for p in parts]
        scores = jnp.einsum('the,she->hts', query, key)
        scores = jnp.where(causal[None], scores, 0.0).astype(jnp.bfloat16).astype(jnp.float32)
        dscores = jnp.einsum('thf,shf->hts', grad, value)
        dscores = jnp.where(causal[None], dscores, 0.0).astype(jnp.bfloat16).astype(jnp.float32)
        attended = jnp.einsum('the,hef->thf', query, state_c) + jnp.einsum('hts,shf->thf', scores, value)
        query_g = jnp.einsum('thf,hef->the', grad, state_c) + jnp.einsum('hts,she->the', dscores, key)
        key_g = jnp.einsum('shf,hef->she', value, adjoint_c) + jnp.einsum('hts,the->she', dscores, query)
        value_g = jnp.einsum('she,hef->shf', key, adjoint_c) + jnp.einsum('hts,thf->shf', scores, grad)
        return (attended.astype(jnp.bfloat16), query_g.astype(jnp.bfloat16),
                key_g.astype(jnp.bfloat16), value_g.astype(jnp.bfloat16))

    attended, query_g, key_g, value_g = lax.map(one_block, (query_b, key_b, value_b, grad_b, state, adjoint))
    attended = attended.reshape(tok_all, col_width)
    weight_grad = jnp.dot(attended.T, cotangent, preferred_element_type=jnp.float32)
    return (query_g.reshape(tok_all, col_width), key_g.reshape(tok_all, col_width),
            value_g.reshape(tok_all, col_width), weight_grad)
```

```python
import jax
import jax.numpy as jnp
from jax import lax
from jax.experimental import pallas as pl
from jax.experimental.pallas import tpu as pltpu
from jax.sharding import PartitionSpec as P

MESH = pl.DeviceIdType.MESH
BF = jnp.bfloat16
F32 = jnp.float32
VM = pltpu.VMEM
DMA = pltpu.SemaphoreType.DMA


def nn(a, b):
    return lax.dot_general(a, b, (((1,), (0,)), ((), ())), preferred_element_type=F32)


def nt(a, b):
    return lax.dot_general(a, b, (((1,), (1,)), ((), ())), preferred_element_type=F32)


def tn(a, b):
    return lax.dot_general(a, b, (((0,), (0,)), ((), ())), preferred_element_type=F32)


def head(h):
    return pl.ds(pl.multiple_of(h * 128, 128), 128)


def loop(lo, hi, body):
    def step(i, carry):
        body(i)
        return carry

    lax.fori_loop(lo, hi, step, 0)


class Place:
    def __init__(self):
        self.me = lax.axis_index("ctx")
        self.tp = lax.axis_index("tp")
        self.p = self.me % 4
        self.core = self.me % 2
        self.zy = self.me // 4
        self.z = self.me // 16
        self.y = self.zy % 4
        self.base = self.me - self.p

    def group(self, p):
        return (self.base + p, self.tp)

    def plane(self, zy):
        return (zy * 4 + self.p, self.tp)

    def along_y(self, y):
        return (self.me + (y - self.y) * 4, self.tp)

    def along_z(self, z):
        return (self.me + (z - self.z) * 16, self.tp)


def remote(src, dst, send, recv, device):
    return pltpu.make_async_remote_copy(
        src_ref=src, dst_ref=dst, send_sem=send, recv_sem=recv, device_id=device, device_id_type=MESH
    )


class Scan:
    def __init__(self, at, refs, reverse):
        self.at, self.reverse = at, reverse
        (self.s, self.a, self.t, self.b, self.pre, self.c, self.d, self.st, self.ga, self.gd, self.pb, self.pc) = refs

    def up_group(self, k):
        q = (self.at.p + k) % 4
        return remote(
            self.s.at[pl.ds(q * 4, 4)], self.a.at[self.at.p], self.ga.at[0, k - 1], self.ga.at[1, k - 1], self.at.group(q)
        )

    def send_up_group(self):
        for k in range(1, 4):
            self.up_group(k).start()
        self.a[self.at.p] = self.s[pl.ds(self.at.p * 4, 4)]

    def up_plane(self, k):
        j = (self.at.zy + k) % 16
        return remote(self.t.at[j], self.b.at[self.at.zy], self.pb.at[0], self.pb.at[1], self.at.plane(j))

    def send_up_plane(self):
        for k in range(1, 4):
            self.up_group(k).wait()
        for h in range(4):
            total = self.a[0, h].astype(F32)
            for q in range(1, 4):
                total = total + self.a[q, h].astype(F32)
            self.t[pl.ds(4 * h, 4)] = total.reshape(4, 32, 128)
        loop(1, 16, lambda k: self.up_plane(k).start())
        self.b[self.at.zy] = self.t[self.at.zy]

    def down_plane(self, k):
        j = (self.at.zy + k) % 16
        return remote(self.pre.at[j], self.c.at[self.at.zy], self.pc.at[0], self.pc.at[1], self.at.plane(j))

    def wait_all(self, src, dst, sems):
        pltpu.make_async_copy(src.at[pl.ds(0, 15)], src.at[pl.ds(0, 15)], sems.at[0]).wait()
        pltpu.make_async_copy(dst.at[pl.ds(0, 15)], dst.at[pl.ds(0, 15)], sems.at[1]).wait()

    def send_down_plane(self):
        self.wait_all(self.t, self.b, self.pb)
        run = jnp.zeros((32, 128), F32)
        for i in reversed(range(16)) if self.reverse else range(16):
            self.pre[i] = run
            run = run + self.b[i]
        loop(1, 16, lambda k: self.down_plane(k).start())
        self.c[self.at.zy] = self.pre[self.at.zy]

    def down_group(self, k):
        q = (self.at.p + k) % 4
        return remote(
            self.d.at[q], self.st.at[pl.ds(self.at.p * 4, 4)], self.gd.at[0, k - 1], self.gd.at[1, k - 1], self.at.group(q)
        )

    def send_down_group(self, memory):
        self.wait_all(self.pre, self.c, self.pc)
        for h in range(4):
            run = self.c[pl.ds(4 * h, 4)].reshape(128, 128)
            if memory is not None:
                run = run + memory[h]
            for q in reversed(range(4)) if self.reverse else range(4):
                self.d[q, h] = run.astype(BF)
                run = run + self.a[q, h].astype(F32)
        for k in range(1, 4):
            self.down_group(k).start()
        self.st[pl.ds(self.at.p * 4, 4)] = self.d[self.at.p]

    def finish(self):
        for k in range(1, 4):
            self.down_group(k).wait()


class Ring:
    def __init__(self, src, land, sems, pos, device):
        self.src, self.land, self.sems, self.pos = src, land, sems, pos
        self.quarters = [pos, (pos + 1) % 4, (pos + 2) % 4, (pos + 3) % 4]
        self.device = device

    def copy(self, way, slot):
        near = self.quarters[1] if way == 0 else self.quarters[3]
        if slot == 0:
            src = self.src.at[self.quarters[2], way]
        elif slot == 1:
            src = self.src.at[near, 1 - way]
        else:
            src = self.src.at[near, way]
        return remote(
            src, self.land.at[way, slot], self.sems.at[0, way, slot], self.sems.at[1, way, slot], self.device(near)
        )

    def send_far(self):
        self.copy(0, 0).start()
        self.copy(1, 0).start()

    def send_near(self, way):
        self.copy(way, 1).start()

    def relay(self, way):
        near = self.quarters[1] if way == 0 else self.quarters[3]
        self.copy(way, 0).wait()
        self.src[near, way] = (self.src[near, way].astype(F32) + self.land[way, 0].astype(F32)).astype(BF)
        self.copy(way, 2).start()

    def result(self, half):
        own = self.src[self.pos, half].astype(F32)
        for way in range(2):
            slot = 2 if way == half else 1
            own = own + self.land[way, slot].astype(F32)
        return own

    def wait_results(self):
        for way in range(2):
            self.copy(way, 1).wait()
            self.copy(way, 2).wait()


def kernel(
    q_hbm, k_hbm, v_hbm, cot_hbm, w_hbm, mem_hbm,
    qg_hbm, kg_hbm, vg_hbm, wg_hbm,
    q, k, v, w, cot, pcot, mem, gacc, g, intra,
    kv_refs, qd_refs,
    att, pa, pb, land_a1, land_b1, s1a, s1b, land_a2, land_b2, fin, fin_land,
    qg, kg, vg, wg,
    in_sem, out_sem, tp_sem, pc_sem, at_sem, ring_sem, fin_sem,
):
    at = Place()
    me, tp, core = at.me, at.tp, at.core
    peer_core = (at.base + (at.p + 1 - 2 * core), tp)
    peer_tp = (me, 1 - tp)

    loads = [
        pltpu.make_async_copy(k_hbm, k, in_sem.at[0]),
        pltpu.make_async_copy(v_hbm, v, in_sem.at[1]),
        pltpu.make_async_copy(q_hbm, q, in_sem.at[2]),
        pltpu.make_async_copy(cot_hbm, cot.at[tp], in_sem.at[3]),
        pltpu.make_async_copy(w_hbm.at[:, pl.ds(0, 1024)], w.at[0], in_sem.at[4]),
        pltpu.make_async_copy(w_hbm.at[:, pl.ds(1024, 1024)], w.at[1], in_sem.at[5]),
        pltpu.make_async_copy(mem_hbm.at[pl.ds(at.p * 4, 4)], mem, in_sem.at[6]),
    ]
    for load in loads:
        load.start()

    barrier = pltpu.get_barrier_semaphore()

    def signal(device):
        pl.semaphore_signal(barrier, inc=1, device_id=device, device_id_type=MESH)

    signal(peer_tp)
    for i in range(1, 4):
        signal(at.group((at.p + i) % 4))
    loop(1, 16, lambda i: signal(at.plane((at.zy + i) % 16)))
    pl.semaphore_wait(barrier, 19)

    cot_copy = remote(cot_hbm, cot.at[tp], tp_sem.at[0], tp_sem.at[1], peer_tp)
    cot_copy.start()

    kv = Scan(at, kv_refs, False)
    qd = Scan(at, qd_refs, True)

    loads[0].wait()
    loads[1].wait()

    def kv_sum(h):
        kv.s[h] = tn(k[:, head(h)], v[:, head(h)]).astype(BF)

    loop(0, 16, kv_sum)
    kv.send_up_group()

    loads[2].wait()
    row = lax.broadcasted_iota(jnp.int32, (256, 256), 0)
    col = lax.broadcasted_iota(jnp.int32, (256, 256), 1)

    def lower(x):
        return jnp.where(row >= col, x, 0.0).astype(BF)

    def upper(x):
        return jnp.where(row <= col, x, 0.0).astype(BF)

    top, low = pl.ds(0, 256), pl.ds(256, 256)

    def causal(a, b, c, h):
        hs = head(h)
        a0, a1, b0, b1, c0, c1 = a[top, hs], a[low, hs], b[top, hs], b[low, hs], c[top, hs], c[low, hs]
        first = nn(lower(nt(a0, b0)), c0)
        second = nn(nt(a1, b0).astype(BF), c0) + nn(lower(nt(a1, b1)), c1)
        return first, second

    def anti(b, a, c, h):
        hs = head(h)
        a0, a1, b0, b1, c0, c1 = a[top, hs], a[low, hs], b[top, hs], b[low, hs], c[top, hs], c[low, hs]
        first = nn(upper(nt(b0, a0)), c0) + nn(nt(b0, a1).astype(BF), c1)
        second = nn(upper(nt(b1, a1)), c1)
        return first, second

    def scored(h):
        first, second = causal(q, k, v, h)
        intra[h, top] = first
        intra[h, low] = second

    loop(0, 8, scored)
    kv.send_up_plane()
    loop(8, 16, scored)

    loads[3].wait()
    loads[4].wait()
    loads[5].wait()

    def wrows(n):
        return pl.ds(pl.multiple_of(n * 256, 256), 256)

    def grad_own(n):
        gacc[:, wrows(n)] = nt(cot[tp], w[tp, wrows(n), :])

    loop(0, 4, grad_own)
    kv.send_down_plane()
    loop(4, 8, grad_own)

    loads[6].wait()
    kv.send_down_group(mem)

    cot_copy.wait()
    pcot_copy = remote(cot.at[1 - core], pcot, pc_sem.at[0], pc_sem.at[1], peer_core)
    pcot_copy.start()

    def grad_other(n):
        g[:, wrows(n)] = (gacc[:, wrows(n)] + nt(cot[1 - tp], w[1 - tp, wrows(n), :])).astype(BF)

    loop(0, 8, grad_other)

    def qd_sum(h):
        qd.s[h] = tn(q[:, head(h)], g[:, head(h)]).astype(BF)

    loop(0, 16, qd_sum)
    qd.send_up_group()

    kv.finish()

    def attend(h):
        a = intra[h] + nn(q[:, head(h)], kv.st[h])
        att[0, h // 4, h % 4] = a.T.astype(BF)

    att_copies = []
    for i in range(4):
        loop(4 * i, 4 * i + 4, attend)
        att_copies.append(remote(att.at[0, i], att.at[1, i], at_sem.at[0, i], at_sem.at[1, i], peer_core))
        att_copies[i].start()

    qd.send_up_plane()

    pcot_copy.wait()
    for copy in att_copies:
        copy.wait()

    y, z = at.y, at.z
    ring_a1 = Ring(pa, land_a1, ring_sem.at[0], y, at.along_y)
    ring_b1 = Ring(pb, land_b1, ring_sem.at[1], z, at.along_z)
    ring_a2 = Ring(s1a, land_a2, ring_sem.at[2], z, at.along_z)
    ring_b2 = Ring(s1b, land_b2, ring_sem.at[3], y, at.along_y)

    def part_a(i):
        yq = ring_a1.quarters[i]
        cols = pl.ds(0, 512)
        r = nn(att[0, :, yq].reshape(512, 512), cot[core, :, cols])
        r = r + nn(att[1, :, yq].reshape(512, 512), pcot[:, cols])
        pa[yq] = r.astype(BF).reshape(2, 2, 128, 512)

    def part_b(i):
        zq = ring_b1.quarters[i]
        cols = pl.ds(512, 512)
        r = nn(att[0, zq].reshape(512, 512), cot[core, :, cols])
        r = r + nn(att[1, zq].reshape(512, 512), pcot[:, cols])
        pb[zq] = r.astype(BF).reshape(2, 2, 128, 512)

    part_a(2)
    ring_a1.send_far()
    part_b(2)
    ring_b1.send_far()
    qd.send_down_plane()
    for way, i in ((0, 1), (1, 3)):
        part_a(i)
        ring_a1.send_near(way)
        part_b(i)
        ring_b1.send_near(way)
    part_a(0)
    part_b(0)
    for ring in (ring_a1, ring_b1):
        for way in range(2):
            ring.relay(way)
    qd.send_down_group(None)

    def query_grad(h):
        hs = head(h)
        first, second = causal(g, v, k, h)
        qg[top, hs] = (first + nt(g[top, hs], kv.st[h])).astype(BF)
        qg[low, hs] = (second + nt(g[low, hs], kv.st[h])).astype(BF)

    loop(0, 16, query_grad)
    outs = [pltpu.make_async_copy(qg, qg_hbm, out_sem.at[0])]
    outs[0].start()

    ring_a1.wait_results()
    ring_b1.wait_results()
    for i in range(4):
        part = ring_a1.result(i // 2) if i % 2 == 0 else part
        s1a[i] = part[i % 2].astype(BF).reshape(2, 64, 512)
    ring_a2.send_far()
    ring_a2.send_near(0)
    ring_a2.send_near(1)
    for i in range(4):
        part = ring_b1.result(i // 2) if i % 2 == 0 else part
        s1b[i] = part[i % 2].astype(BF).reshape(2, 64, 512)
    ring_b2.send_far()
    ring_b2.send_near(0)
    ring_b2.send_near(1)

    qd.finish()

    def key_value(h):
        hs = head(h)
        first, second = anti(v, g, q, h)
        kg[top, hs] = (first + nt(v[top, hs], qd.st[h])).astype(BF)
        kg[low, hs] = (second + nt(v[low, hs], qd.st[h])).astype(BF)
        first, second = anti(k, q, g, h)
        vg[top, hs] = (first + nn(k[top, hs], qd.st[h])).astype(BF)
        vg[low, hs] = (second + nn(k[low, hs], qd.st[h])).astype(BF)

    loop(0, 4, key_value)
    for ring in (ring_a2, ring_b2):
        for way in range(2):
            ring.relay(way)
    loop(4, 8, key_value)
    ring_a2.wait_results()
    ring_b2.wait_results()
    for i, ring in enumerate((ring_a2, ring_b2)):
        for half in range(2):
            part = ring.result(half).astype(BF)
            for j in range(2):
                fin[half * 2 + j, :, pl.ds(512 * i, 512)] = part[32 * j : 32 * j + 32]

    def last(i):
        r = (at.p + i) % 4
        return remote(fin.at[r], fin_land.at[at.p], fin_sem.at[0, i - 1], fin_sem.at[1, i - 1], at.group(r))

    for i in range(1, 4):
        last(i).start()
    fin_land[at.p] = fin[at.p]
    loop(8, 16, key_value)
    outs.append(pltpu.make_async_copy(kg, kg_hbm, out_sem.at[1]))
    outs[1].start()
    outs.append(pltpu.make_async_copy(vg, vg_hbm, out_sem.at[2]))
    outs[2].start()
    for i in range(1, 4):
        last(i).wait()
    for d in range(2):
        wg[:, pl.ds(1024 * d, 1024)] = fin_land[d].astype(F32) + fin_land[2 + d].astype(F32)
    outs.append(pltpu.make_async_copy(wg, wg_hbm, out_sem.at[3]))
    outs[3].start()
    for out in outs:
        out.wait()


def scan_scratch():
    return (
        VM((16, 128, 128), BF),
        VM((4, 4, 128, 128), BF),
        VM((16, 32, 128), F32),
        VM((16, 32, 128), F32),
        VM((16, 32, 128), F32),
        VM((16, 32, 128), F32),
        VM((4, 4, 128, 128), BF),
        VM((16, 128, 128), BF),
        DMA((2, 3)),
        DMA((2, 3)),
        DMA((2,)),
        DMA((2,)),
    )


def local(queries, keys, values, cotangent, out_weight, memory):
    tok = VM((512, 2048), BF)
    any_spec = pl.BlockSpec(memory_space=pl.ANY)
    like = jax.ShapeDtypeStruct((512, 2048), BF)
    return pl.pallas_call(
        kernel,
        out_shape=(like, like, like, jax.ShapeDtypeStruct((32, 2048), F32)),
        in_specs=[any_spec] * 6,
        out_specs=(any_spec,) * 4,
        scratch_shapes=[
            tok, tok, tok,
            VM((2, 2048, 1024), BF),
            VM((2, 512, 1024), BF),
            VM((512, 1024), BF),
            VM((4, 128, 128), F32),
            VM((512, 2048), F32),
            tok,
            VM((16, 512, 128), F32),
            scan_scratch(),
            scan_scratch(),
            VM((2, 4, 4, 128, 512), BF),
            VM((4, 2, 2, 128, 512), BF),
            VM((4, 2, 2, 128, 512), BF),
            VM((2, 3, 2, 128, 512), BF),
            VM((2, 3, 2, 128, 512), BF),
            VM((4, 2, 64, 512), BF),
            VM((4, 2, 64, 512), BF),
            VM((2, 3, 64, 512), BF),
            VM((2, 3, 64, 512), BF),
            VM((4, 32, 1024), BF),
            VM((4, 32, 1024), BF),
            tok, tok, tok,
            VM((32, 2048), F32),
            DMA((7,)),
            DMA((4,)),
            DMA((2,)),
            DMA((2,)),
            DMA((2, 4)),
            DMA((4, 2, 2, 3)),
            DMA((2, 3)),
        ],
        compiler_params=pltpu.CompilerParams(
            collective_id=0, has_side_effects=True, vmem_limit_bytes=67043328
        ),
    )(queries, keys, values, cotangent, out_weight, memory)


def solution(mesh):
    in_specs = (
        P("ctx", "tp"),
        P("ctx", "tp"),
        P("ctx", "tp"),
        P("ctx", "tp"),
        P("tp", None),
        P("tp", None, None),
    )
    out_specs = (P("ctx", "tp"), P("ctx", "tp"), P("ctx", "tp"), P(("tp", "ctx"), None))
    return jax.shard_map(local, mesh=mesh, in_specs=in_specs, out_specs=out_specs, check_vma=False)
```

```python
import jax
import jax.numpy as jnp
from jax import lax
from jax.experimental import pallas as pl
from jax.experimental.pallas import tpu as pltpu
from jax.sharding import PartitionSpec as P

MESH = pl.DeviceIdType.MESH
BF = jnp.bfloat16
F32 = jnp.float32
VM = pltpu.VMEM
DMA = pltpu.SemaphoreType.DMA


def nn(a, b):
    return lax.dot_general(a, b, (((1,), (0,)), ((), ())), preferred_element_type=F32)


def nt(a, b):
    return lax.dot_general(a, b, (((1,), (1,)), ((), ())), preferred_element_type=F32)


def tn(a, b):
    return lax.dot_general(a, b, (((0,), (0,)), ((), ())), preferred_element_type=F32)


def head(h):
    return pl.ds(pl.multiple_of(h * 128, 128), 128)


def loop(lo, hi, body):
    side = 4 if (hi - lo) % 4 == 0 else 2

    def step(i, carry):
        for j in range(side):
            body(lo + side * i + j)
        return carry

    lax.fori_loop(0, (hi - lo) // side, step, 0)


def each(lo, hi, body):
    def step(i, carry):
        body(i)
        return carry

    lax.fori_loop(lo, hi, step, 0)


class Place:
    def __init__(self):
        self.me = lax.axis_index("ctx")
        self.tp = lax.axis_index("tp")
        self.p = self.me % 4
        self.core = self.me % 2
        self.x = self.p // 2
        self.zy = self.me // 4
        self.z = self.me // 16
        self.y = self.zy % 4
        self.base = self.me - self.p

    def other_core(self):
        return (self.base + 2 * self.x + 1 - self.core, self.tp)

    def other_x(self):
        return (self.base + 2 * (1 - self.x) + self.core, self.tp)

    def group(self, p):
        return (self.base + p, self.tp)

    def plane(self, zy):
        return (zy * 4 + self.p, self.tp)

    def along_y(self, y):
        return (self.me + (y - self.y) * 4, self.tp)

    def along_z(self, z):
        return (self.me + (z - self.z) * 16, self.tp)


def remote(src, dst, send, recv, device):
    return pltpu.make_async_remote_copy(
        src_ref=src, dst_ref=dst, send_sem=send, recv_sem=recv, device_id=device, device_id_type=MESH
    )


class Scan:
    def __init__(self, at, refs, reverse):
        self.at, self.reverse = at, reverse
        (self.s, self.a, self.pc, self.px, self.t, self.b, self.pre, self.c, self.e, self.f, self.d, self.st,
         self.sem, self.up, self.down) = refs
        self.copies = [
            remote(self.s.at[pl.ds(8 * (1 - at.core), 8)], self.a, self.sem.at[0, 0], self.sem.at[1, 0], at.other_core()),
            remote(self.pc.at[1 - at.x], self.px, self.sem.at[0, 1], self.sem.at[1, 1], at.other_x()),
            remote(self.e, self.f, self.sem.at[0, 2], self.sem.at[1, 2], at.other_x()),
            remote(self.d, self.st.at[pl.ds(8 * at.core, 8)], self.sem.at[0, 3], self.sem.at[1, 3], at.other_core()),
        ]

    def send_core(self):
        self.copies[0].start()

    def send_x(self):
        self.copies[0].wait()
        for i in range(2):
            for h in range(4):
                own = self.s[8 * self.at.core + 4 * i + h].astype(F32)
                self.pc[i, h] = (own + self.a[4 * i + h].astype(F32)).astype(BF)
        self.copies[1].start()

    def up_plane(self, k):
        j = (self.at.zy + k) % 16
        return remote(self.t.at[j], self.b.at[self.at.zy], self.up.at[0], self.up.at[1], self.at.plane(j))

    def send_up(self):
        self.copies[1].wait()
        for h in range(4):
            total = self.pc[self.at.x, h].astype(F32) + self.px[h].astype(F32)
            self.t[pl.ds(4 * h, 4)] = total.reshape(4, 32, 128)
        each(1, 16, lambda k: self.up_plane(k).start())
        self.b[self.at.zy] = self.t[self.at.zy]

    def down_plane(self, k):
        j = (self.at.zy + k) % 16
        return remote(self.pre.at[j], self.c.at[self.at.zy], self.down.at[0], self.down.at[1], self.at.plane(j))

    def wait_all(self, src, dst, sems):
        pltpu.make_async_copy(src.at[pl.ds(0, 15)], src.at[pl.ds(0, 15)], sems.at[0]).wait()
        pltpu.make_async_copy(dst.at[pl.ds(0, 15)], dst.at[pl.ds(0, 15)], sems.at[1]).wait()

    def send_down(self):
        self.wait_all(self.t, self.b, self.up)
        run = jnp.zeros((32, 128), F32)
        for i in reversed(range(16)) if self.reverse else range(16):
            self.pre[i] = run
            run = run + self.b[i]
        each(1, 16, lambda k: self.down_plane(k).start())
        self.c[self.at.zy] = self.pre[self.at.zy]

    def send_back_x(self, memory):
        self.wait_all(self.pre, self.c, self.down)
        after = self.at.x == (0 if self.reverse else 1)
        for h in range(4):
            run = self.c[pl.ds(4 * h, 4)].reshape(128, 128)
            if memory is not None:
                run = run + memory[h]
            mine, theirs = self.pc[self.at.x, h].astype(F32), self.px[h].astype(F32)
            self.e[h] = (run + jnp.where(after, 0.0, mine)).astype(BF)
            self.c[pl.ds(4 * h, 4)] = (run + jnp.where(after, theirs, 0.0)).reshape(4, 32, 128)
        self.copies[2].start()

    def send_back_core(self):
        self.copies[2].wait()
        after = self.at.core == (0 if self.reverse else 1)
        first = 8 * self.at.core

        def settle(run, h):
            mine, theirs = self.s[first + h].astype(F32), self.a[h].astype(F32)
            self.d[h] = (run + jnp.where(after, 0.0, mine)).astype(BF)
            self.st[first + h] = (run + jnp.where(after, theirs, 0.0)).astype(BF)

        for h in range(4):
            settle(self.c[pl.ds(4 * h, 4)].reshape(128, 128), 4 * self.at.x + h)
            settle(self.f[h].astype(F32), 4 * (1 - self.at.x) + h)
        self.copies[3].start()

    def finish(self):
        self.copies[3].wait()


class Ring:
    def __init__(self, src, land, sems, pos, device):
        self.src, self.land, self.sems, self.pos = src, land, sems, pos
        self.quarters = [pos, (pos + 1) % 4, (pos + 2) % 4, (pos + 3) % 4]
        self.device = device

    def copy(self, way, slot):
        near = self.quarters[1] if way == 0 else self.quarters[3]
        if slot == 0:
            src = self.src.at[self.quarters[2], way]
        elif slot == 1:
            src = self.src.at[near, 1 - way]
        else:
            src = self.src.at[near, way]
        return remote(
            src, self.land.at[way, slot], self.sems.at[0, way, slot], self.sems.at[1, way, slot], self.device(near)
        )

    def send_far(self):
        self.copy(0, 0).start()
        self.copy(1, 0).start()

    def send_near(self, way):
        self.copy(way, 1).start()

    def relay(self, way):
        near = self.quarters[1] if way == 0 else self.quarters[3]
        self.copy(way, 0).wait()
        self.src[near, way] = (self.src[near, way].astype(F32) + self.land[way, 0].astype(F32)).astype(BF)
        self.copy(way, 2).start()

    def result(self, half):
        own = self.src[self.pos, half].astype(F32)
        for way in range(2):
            slot = 2 if way == half else 1
            own = own + self.land[way, slot].astype(F32)
        return own

    def wait_results(self):
        for way in range(2):
            self.copy(way, 1).wait()
            self.copy(way, 2).wait()


def kernel(
    q_hbm, k_hbm, v_hbm, cot_hbm, w_hbm, mem_hbm,
    qg, kg, vg, wg,
    q, k, v, w, cot, pcot, mem, gacc, g, intra,
    kv_refs, qd_refs,
    sup, att, pa, pb, land_a1, land_b1, s1a, s1b, land_a2, land_b2, fin, fin_land,
    in_sem, tp_sem, pc_sem, at_sem, ring_sem, fin_sem,
):
    at = Place()
    me, tp, core = at.me, at.tp, at.core
    peer_core = at.other_core()
    peer_tp = (me, 1 - tp)

    loads = [
        pltpu.make_async_copy(k_hbm, k, in_sem.at[0]),
        pltpu.make_async_copy(v_hbm, v, in_sem.at[1]),
        pltpu.make_async_copy(q_hbm, q, in_sem.at[2]),
        pltpu.make_async_copy(cot_hbm, cot.at[tp], in_sem.at[3]),
        pltpu.make_async_copy(w_hbm.at[:, pl.ds(0, 1024)], w.at[0], in_sem.at[4]),
        pltpu.make_async_copy(w_hbm.at[:, pl.ds(1024, 1024)], w.at[1], in_sem.at[5]),
        pltpu.make_async_copy(mem_hbm.at[pl.ds(8 * core + 4 * at.x, 4)], mem, in_sem.at[6]),
    ]
    for load in loads:
        load.start()

    barrier = pltpu.get_barrier_semaphore()

    def signal(device):
        pl.semaphore_signal(barrier, inc=1, device_id=device, device_id_type=MESH)

    signal(peer_tp)
    for i in range(1, 4):
        signal(at.group((at.p + i) % 4))
    each(1, 16, lambda i: signal(at.plane((at.zy + i) % 16)))

    def mine(c):
        return pl.ds(pl.multiple_of(c * 512, 512), 512)

    cot_copies = [
        remote(cot_hbm.at[rows], cot.at[tp, rows], tp_sem.at[0, i], tp_sem.at[1, i], peer_tp)
        for i, rows in enumerate((pl.ds(0, 64), pl.ds(64, 192), pl.ds(256, 128), pl.ds(384, 128)))
    ]
    near_cot = remote(cot_hbm.at[:, mine(1 - core)], pcot.at[0], pc_sem.at[0, 0], pc_sem.at[1, 0], peer_core)
    far_cot = remote(cot.at[1 - tp, :, mine(1 - core)], pcot.at[1], pc_sem.at[0, 1], pc_sem.at[1, 1], peer_core)

    kv = Scan(at, kv_refs, False)
    qd = Scan(at, qd_refs, True)

    loads[0].wait()
    loads[1].wait()

    def kv_sum(h):
        kv.s[h] = tn(k[:, head(h)], v[:, head(h)]).astype(BF)

    loop(0, 16, kv_sum)
    pl.semaphore_wait(barrier, 19)
    kv.send_core()
    cot_copies[0].start()
    near_cot.start()

    loads[2].wait()
    row = lax.broadcasted_iota(jnp.int32, (256, 256), 0)
    col = lax.broadcasted_iota(jnp.int32, (256, 256), 1)

    def lower(x):
        return jnp.where(row >= col, x, 0.0).astype(BF)

    def upper(x):
        return jnp.where(row <= col, x, 0.0).astype(BF)

    top, low = pl.ds(0, 256), pl.ds(256, 256)

    def causal(a, b, c, h):
        hs = head(h)
        a0, a1, b0, b1, c0, c1 = a[top, hs], a[low, hs], b[top, hs], b[low, hs], c[top, hs], c[low, hs]
        first = nn(lower(nt(a0, b0)), c0)
        second = nn(nt(a1, b0).astype(BF), c0) + nn(lower(nt(a1, b1)), c1)
        return first, second

    def anti(b, a, c, h):
        hs = head(h)
        a0, a1, b0, b1, c0, c1 = a[top, hs], a[low, hs], b[top, hs], b[low, hs], c[top, hs], c[low, hs]
        first = nn(upper(nt(b0, a0)), c0) + nn(nt(b0, a1).astype(BF), c1)
        second = nn(upper(nt(b1, a1)), c1)
        return first, second

    def scored(h):
        first, second = causal(q, k, v, h)
        intra[h, top] = first
        intra[h, low] = second

    def turned(h):
        hs = head(h)
        k0, k1, q0, q1 = k[top, hs], k[low, hs], q[top, hs], q[low, hs]
        sup[h, 0] = upper(nt(k0, q0))
        sup[h, 1] = nt(k0, q1).astype(BF)
        sup[h, 2] = upper(nt(k1, q1))

    loop(0, 4, scored)
    kv.send_x()
    cot_copies[1].start()
    cot_copies[2].start()
    loop(4, 16, scored)
    kv.send_up()

    for load in loads[3:6]:
        load.wait()

    def wrows(n):
        return pl.ds(pl.multiple_of(n * 256, 256), 256)

    def grad_own(n):
        gacc[:, wrows(n)] = nt(cot[tp], w[tp, wrows(n), :])

    each(0, 8, grad_own)
    loop(0, 8, turned)
    kv.send_down()

    def grad_top(n):
        g[top, wrows(n)] = (gacc[top, wrows(n)] + nt(cot[1 - tp, top, :], w[1 - tp, wrows(n), :])).astype(BF)

    def grad_low(n):
        g[low, wrows(n)] = (gacc[low, wrows(n)] + nt(cot[1 - tp, low, :], w[1 - tp, wrows(n), :])).astype(BF)

    loads[6].wait()
    cot_copies[0].wait()
    cot_copies[1].wait()
    each(0, 8, grad_top)
    kv.send_back_x(mem)
    cot_copies[3].start()
    loop(8, 16, turned)
    kv.send_back_core()
    kv.finish()

    def attend(h):
        a = intra[h] + nn(q[:, head(h)], kv.st[h])
        att[0, h // 4, h % 4] = a.T.astype(BF)

    att_copies = []
    for i in range(4):
        loop(4 * i, 4 * i + 4, attend)
        att_copies.append(remote(att.at[0, i], att.at[1, i], at_sem.at[0, i], at_sem.at[1, i], peer_core))
        att_copies[i].start()

    def query_top(h):
        hs = head(h)
        g0 = g[top, hs]
        qg[top, hs] = (nn(lower(nt(g0, v[top, hs])), k[top, hs]) + nt(g0, kv.st[h])).astype(BF)

    def query_low(h):
        hs = head(h)
        g1 = g[low, hs]
        r = nn(nt(g1, v[top, hs]).astype(BF), k[top, hs]) + nn(lower(nt(g1, v[low, hs])), k[low, hs])
        qg[low, hs] = (r + nt(g1, kv.st[h])).astype(BF)

    loop(0, 16, query_top)
    near_cot.wait()
    for copy in att_copies:
        copy.wait()

    y, z = at.y, at.z
    ring_a1 = Ring(pa, land_a1, ring_sem.at[0], y, at.along_y)
    ring_b1 = Ring(pb, land_b1, ring_sem.at[1], z, at.along_z)
    ring_a2 = Ring(s1a, land_a2, ring_sem.at[2], z, at.along_z)
    ring_b2 = Ring(s1b, land_b2, ring_sem.at[3], y, at.along_y)

    def part_a(i):
        yq = ring_a1.quarters[i]
        r = nn(att[0, :, yq].reshape(512, 512), cot[tp, :, mine(core)])
        r = r + nn(att[1, :, yq].reshape(512, 512), pcot[0])
        pa[yq] = r.astype(BF).reshape(2, 2, 128, 512)

    def part_b(i):
        zq = ring_b1.quarters[i]
        r = nn(att[0, zq].reshape(512, 512), cot[1 - tp, :, mine(core)])
        r = r + nn(att[1, zq].reshape(512, 512), pcot[1])
        pb[zq] = r.astype(BF).reshape(2, 2, 128, 512)

    part_a(2)
    ring_a1.send_far()
    cot_copies[2].wait()
    cot_copies[3].wait()
    far_cot.start()
    each(0, 8, grad_low)

    def qd_sum(h):
        qd.s[h] = tn(q[:, head(h)], g[:, head(h)]).astype(BF)

    loop(0, 16, qd_sum)
    qd.send_core()
    far_cot.wait()
    part_b(2)
    ring_b1.send_far()
    part_a(1)
    ring_a1.send_near(0)
    qd.send_x()
    part_a(3)
    ring_a1.send_near(1)
    part_b(1)
    ring_b1.send_near(0)
    part_b(3)
    ring_b1.send_near(1)
    loop(0, 4, query_low)
    qd.send_up()
    ring_a1.relay(0)
    ring_a1.relay(1)
    part_a(0)
    part_b(0)

    def key_scored(h):
        first, second = anti(v, g, q, h)
        intra[h, top] = first
        intra[h, low] = second

    def value_scored(h):
        g0, g1 = g[top, head(h)], g[low, head(h)]
        gacc[top, head(h)] = nn(sup[h, 0], g0) + nn(sup[h, 1], g1)
        gacc[low, head(h)] = nn(sup[h, 2], g1)

    loop(4, 8, query_low)
    ring_b1.relay(0)
    ring_b1.relay(1)
    loop(8, 16, query_low)
    loop(0, 4, key_scored)
    qd.send_down()

    def stage_two(first, second, to):
        first.wait_results()
        for half in range(2):
            part = first.result(half)
            for i in range(2):
                to[2 * half + i] = part[i].astype(BF).reshape(2, 64, 512)
        second.send_far()
        second.send_near(0)
        second.send_near(1)

    loop(4, 8, key_scored)
    stage_two(ring_a1, ring_a2, s1a)
    loop(8, 12, key_scored)
    stage_two(ring_b1, ring_b2, s1b)
    loop(12, 16, key_scored)
    qd.send_back_x(None)
    ring_a2.relay(0)
    ring_a2.relay(1)
    loop(0, 4, value_scored)
    ring_b2.relay(0)
    ring_b2.relay(1)
    loop(4, 12, value_scored)
    qd.send_back_core()
    loop(12, 16, value_scored)
    ring_a2.wait_results()
    ring_b2.wait_results()
    for i, ring in enumerate((ring_a2, ring_b2)):
        for half in range(2):
            part = ring.result(half).astype(BF)
            for j in range(2):
                fin[half * 2 + j, :, pl.ds(512 * i, 512)] = part[32 * j : 32 * j + 32]

    def last(i):
        r = (at.p + i) % 4
        return remote(fin.at[r], fin_land.at[at.p], fin_sem.at[0, i - 1], fin_sem.at[1, i - 1], at.group(r))

    for i in range(1, 4):
        last(i).start()
    fin_land[at.p] = fin[at.p]
    qd.finish()

    def key_grad(h):
        hs = head(h)
        kg[:, hs] = (intra[h] + nt(v[:, hs], qd.st[h])).astype(BF)

    def value_grad(h):
        hs = head(h)
        vg[:, hs] = (gacc[:, hs] + nn(k[:, hs], qd.st[h])).astype(BF)

    loop(0, 16, key_grad)
    loop(0, 16, value_grad)
    for i in range(1, 4):
        last(i).wait()
    for c in range(2):
        r = fin_land[c].astype(F32) + fin_land[2 + c].astype(F32)
        wg[:, pl.ds(pl.multiple_of(tp * 1024 + c * 512, 512), 512)] = r[:, :512]
        wg[:, pl.ds(pl.multiple_of((1 - tp) * 1024 + c * 512, 512), 512)] = r[:, 512:]


def scan_scratch():
    piece = VM((16, 32, 128), F32)
    return (
        VM((16, 128, 128), BF),
        VM((8, 128, 128), BF),
        VM((2, 4, 128, 128), BF),
        VM((4, 128, 128), BF),
        piece, piece, piece, piece,
        VM((4, 128, 128), BF),
        VM((4, 128, 128), BF),
        VM((8, 128, 128), BF),
        VM((16, 128, 128), BF),
        DMA((2, 4)),
        DMA((2,)),
        DMA((2,)),
    )


def local(queries, keys, values, cotangent, out_weight, memory):
    tok = VM((512, 2048), BF)
    any_spec = pl.BlockSpec(memory_space=pl.ANY)
    like = jax.ShapeDtypeStruct((512, 2048), BF)
    return pl.pallas_call(
        kernel,
        out_shape=(VM((512, 2048), BF), VM((512, 2048), BF), VM((512, 2048), BF), VM((32, 2048), F32)),
        in_specs=[any_spec] * 6,
        out_specs=(pl.BlockSpec(memory_space=VM),) * 4,
        scratch_shapes=[
            tok, tok, tok,
            VM((2, 2048, 1024), BF),
            VM((2, 512, 1024), BF),
            VM((2, 512, 512), BF),
            VM((4, 128, 128), F32),
            VM((512, 2048), F32),
            tok,
            VM((16, 512, 128), F32),
            scan_scratch(),
            scan_scratch(),
            VM((16, 3, 256, 256), BF),
            VM((2, 4, 4, 128, 512), BF),
            VM((4, 2, 2, 128, 512), BF),
            VM((4, 2, 2, 128, 512), BF),
            VM((2, 3, 2, 128, 512), BF),
            VM((2, 3, 2, 128, 512), BF),
            VM((4, 2, 64, 512), BF),
            VM((4, 2, 64, 512), BF),
            VM((2, 3, 64, 512), BF),
            VM((2, 3, 64, 512), BF),
            VM((4, 32, 1024), BF),
            VM((4, 32, 1024), BF),
            DMA((7,)),
            DMA((2, 4)),
            DMA((2, 2)),
            DMA((2, 4)),
            DMA((4, 2, 2, 3)),
            DMA((2, 3)),
        ],
        compiler_params=pltpu.CompilerParams(
            collective_id=0, has_side_effects=True, vmem_limit_bytes=59768832
        ),
    )(queries, keys, values, cotangent, out_weight, memory)


def solution(mesh):
    in_specs = (
        P("ctx", "tp"),
        P("ctx", "tp"),
        P("ctx", "tp"),
        P("ctx", "tp"),
        P("tp", None),
        P("tp", None, None),
    )
    out_specs = (P("ctx", "tp"), P("ctx", "tp"), P("ctx", "tp"), P(("tp", "ctx"), None))
    return jax.shard_map(local, mesh=mesh, in_specs=in_specs, out_specs=out_specs, check_vma=False)
```

```python
import jax
import jax.numpy as jnp
from jax import lax
from jax.experimental import pallas as pl
from jax.experimental.pallas import tpu as pltpu
from jax.sharding import PartitionSpec as P

MESH = pl.DeviceIdType.MESH
BF = jnp.bfloat16
F32 = jnp.float32
VM = pltpu.VMEM
DMA = pltpu.SemaphoreType.DMA


def nn(a, b):
    return lax.dot_general(a, b, (((1,), (0,)), ((), ())), preferred_element_type=F32)


def nt(a, b):
    return lax.dot_general(a, b, (((1,), (1,)), ((), ())), preferred_element_type=F32)


def tn(a, b):
    return lax.dot_general(a, b, (((0,), (0,)), ((), ())), preferred_element_type=F32)


def head(h):
    return pl.ds(pl.multiple_of(h * 128, 128), 128)


def loop(lo, hi, body):
    side = 4 if (hi - lo) % 4 == 0 else 2

    def step(i, carry):
        for j in range(side):
            body(lo + side * i + j)
        return carry

    lax.fori_loop(0, (hi - lo) // side, step, 0)


def each(lo, hi, body):
    def step(i, carry):
        body(i)
        return carry

    lax.fori_loop(lo, hi, step, 0)


class Place:
    def __init__(self):
        self.me = lax.axis_index("ctx")
        self.tp = lax.axis_index("tp")
        self.p = self.me % 4
        self.core = self.me % 2
        self.x = self.p // 2
        self.zy = self.me // 4
        self.z = self.me // 16
        self.y = self.zy % 4
        self.base = self.me - self.p

    def other_core(self):
        return (self.base + 2 * self.x + 1 - self.core, self.tp)

    def other_x(self):
        return (self.base + 2 * (1 - self.x) + self.core, self.tp)

    def group(self, p):
        return (self.base + p, self.tp)

    def plane(self, zy):
        return (zy * 4 + self.p, self.tp)

    def along_y(self, y):
        return (self.me + (y - self.y) * 4, self.tp)

    def along_z(self, z):
        return (self.me + (z - self.z) * 16, self.tp)


def remote(src, dst, send, recv, device):
    return pltpu.make_async_remote_copy(
        src_ref=src, dst_ref=dst, send_sem=send, recv_sem=recv, device_id=device, device_id_type=MESH
    )


class Scan:
    def __init__(self, at, refs, reverse):
        self.at, self.reverse = at, reverse
        (self.s, self.a, self.pc, self.px, self.t, self.b, self.pre, self.c, self.run, self.e, self.f, self.d, self.st,
         self.sem, self.up, self.down) = refs
        self.copies = [
            remote(self.s.at[pl.ds(8 * (1 - at.core), 8)], self.a, self.sem.at[0, 0], self.sem.at[1, 0], at.other_core()),
            remote(self.pc.at[1 - at.x], self.px, self.sem.at[0, 1], self.sem.at[1, 1], at.other_x()),
            remote(self.e, self.f, self.sem.at[0, 2], self.sem.at[1, 2], at.other_x()),
            remote(self.d, self.st.at[pl.ds(8 * at.core, 8)], self.sem.at[0, 3], self.sem.at[1, 3], at.other_core()),
        ]

    def send_core(self):
        self.copies[0].start()

    def send_x(self):
        self.copies[0].wait()
        for i in range(2):
            for h in range(4):
                own = self.s[8 * self.at.core + 4 * i + h].astype(F32)
                self.pc[i, h] = (own + self.a[4 * i + h].astype(F32)).astype(BF)
        self.copies[1].start()

    def up_plane(self, k):
        j = (self.at.zy + k) % 16
        return remote(self.t.at[j], self.b.at[self.at.zy], self.up.at[0], self.up.at[1], self.at.plane(j))

    def send_up(self):
        self.copies[1].wait()
        for h in range(4):
            total = self.pc[self.at.x, h].astype(F32) + self.px[h].astype(F32)
            self.t[pl.ds(4 * h, 4)] = total.reshape(4, 32, 128).astype(self.t.dtype)
        each(1, 16, lambda k: self.up_plane(k).start())
        self.b[self.at.zy] = self.t[self.at.zy]

    def down_plane(self, k):
        j = (self.at.zy + k) % 16
        return remote(self.pre.at[j], self.c.at[self.at.zy], self.down.at[0], self.down.at[1], self.at.plane(j))

    def wait_all(self, src, dst, sems):
        pltpu.make_async_copy(src.at[pl.ds(0, 15)], src.at[pl.ds(0, 15)], sems.at[0]).wait()
        pltpu.make_async_copy(dst.at[pl.ds(0, 15)], dst.at[pl.ds(0, 15)], sems.at[1]).wait()

    def send_down(self):
        self.wait_all(self.t, self.b, self.up)
        run = jnp.zeros((32, 128), F32)
        for i in reversed(range(16)) if self.reverse else range(16):
            self.pre[i] = run.astype(self.pre.dtype)
            run = run + self.b[i].astype(F32)
        each(1, 16, lambda k: self.down_plane(k).start())
        self.c[self.at.zy] = self.pre[self.at.zy]

    def send_back_x(self, memory):
        self.wait_all(self.pre, self.c, self.down)
        after = self.at.x == (0 if self.reverse else 1)
        for h in range(4):
            run = self.c[pl.ds(4 * h, 4)].astype(F32).reshape(128, 128)
            if memory is not None:
                run = run + memory[h]
            mine, theirs = self.pc[self.at.x, h].astype(F32), self.px[h].astype(F32)
            self.e[h] = (run + jnp.where(after, 0.0, mine)).astype(BF)
            self.run[h] = run + jnp.where(after, theirs, 0.0)
        self.copies[2].start()

    def send_back_core(self):
        self.copies[2].wait()
        after = self.at.core == (0 if self.reverse else 1)
        first = 8 * self.at.core

        def settle(run, h):
            mine, theirs = self.s[first + h].astype(F32), self.a[h].astype(F32)
            self.d[h] = (run + jnp.where(after, 0.0, mine)).astype(BF)
            self.st[first + h] = (run + jnp.where(after, theirs, 0.0)).astype(BF)

        for h in range(4):
            settle(self.run[h], 4 * self.at.x + h)
            settle(self.f[h].astype(F32), 4 * (1 - self.at.x) + h)
        self.copies[3].start()

    def finish(self):
        self.copies[3].wait()


class Ring:
    def __init__(self, src, land, sems, pos, device):
        self.src, self.land, self.sems, self.pos = src, land, sems, pos
        self.quarters = [pos, (pos + 1) % 4, (pos + 2) % 4, (pos + 3) % 4]
        self.device = device

    def copy(self, way, slot):
        near = self.quarters[1] if way == 0 else self.quarters[3]
        if slot == 0:
            src = self.src.at[self.quarters[2], way]
        elif slot == 1:
            src = self.src.at[near, 1 - way]
        else:
            src = self.src.at[near, way]
        return remote(
            src, self.land.at[way, slot], self.sems.at[0, way, slot], self.sems.at[1, way, slot], self.device(near)
        )

    def send_far(self):
        self.copy(0, 0).start()
        self.copy(1, 0).start()

    def send_near(self, way):
        self.copy(way, 1).start()

    def relay(self, way):
        near = self.quarters[1] if way == 0 else self.quarters[3]
        self.copy(way, 0).wait()
        self.src[near, way] = (self.src[near, way].astype(F32) + self.land[way, 0].astype(F32)).astype(BF)
        self.copy(way, 2).start()

    def result(self, half):
        own = self.src[self.pos, half].astype(F32)
        for way in range(2):
            slot = 2 if way == half else 1
            own = own + self.land[way, slot].astype(F32)
        return own

    def wait_results(self):
        for way in range(2):
            self.copy(way, 1).wait()
            self.copy(way, 2).wait()


def kernel(
    q_hbm, k_hbm, v_hbm, cot_hbm, w_hbm, mem_hbm,
    qg, kg, vg, wg,
    q, k, v, w, cot, pcot, mem, gacc, g, intra,
    kv_refs, qd_refs,
    sup, qacc, att, parts, lands, s1a, s1b, land_a2, land_b2, fin, fin_land,
    in_sem, tp_sem, pc_sem, at_sem, ring_sem, fin_sem,
):
    at = Place()
    me, tp, core = at.me, at.tp, at.core
    peer_core = at.other_core()
    peer_tp = (me, 1 - tp)

    loads = [
        pltpu.make_async_copy(q_hbm, q, in_sem.at[2]),
        pltpu.make_async_copy(cot_hbm, cot.at[tp], in_sem.at[3]),
        pltpu.make_async_copy(w_hbm.at[:, pl.ds(0, 1024)], w.at[0], in_sem.at[4]),
        pltpu.make_async_copy(w_hbm.at[:, pl.ds(1024, 1024)], w.at[1], in_sem.at[5]),
        pltpu.make_async_copy(mem_hbm.at[pl.ds(8 * core + 4 * at.x, 4)], mem, in_sem.at[6]),
    ]
    def block(src, dst, i, sem):
        return pltpu.make_async_copy(src.at[:, pl.ds(512 * i, 512)], dst.at[:, pl.ds(512 * i, 512)], in_sem.at[sem])

    block_loads = [(block(k_hbm, k, i, 7 + i), block(v_hbm, v, i, 11 + i)) for i in range(4)]
    for pair in block_loads:
        pair[0].start()
        pair[1].start()
    for load in loads:
        load.start()

    barrier = pltpu.get_barrier_semaphore()

    def signal(device):
        pl.semaphore_signal(barrier, inc=1, device_id=device, device_id_type=MESH)

    signal(peer_tp)
    for i in range(1, 4):
        signal(at.group((at.p + i) % 4))
    each(1, 16, lambda i: signal(at.plane((at.zy + i) % 16)))

    def mine(c):
        return pl.ds(pl.multiple_of(c * 512, 512), 512)

    cot_copies = [
        remote(cot_hbm.at[rows], cot.at[tp, rows], tp_sem.at[0, i], tp_sem.at[1, i], peer_tp)
        for i, rows in enumerate((pl.ds(0, 64), pl.ds(64, 192), pl.ds(256, 64), pl.ds(320, 192)))
    ]
    near_cot = remote(cot_hbm.at[:, mine(1 - core)], pcot.at[0], pc_sem.at[0, 0], pc_sem.at[1, 0], peer_core)
    far_cot = remote(cot.at[1 - tp, :, mine(1 - core)], pcot.at[1], pc_sem.at[0, 1], pc_sem.at[1, 1], peer_core)

    kv = Scan(at, kv_refs, False)
    qd = Scan(at, qd_refs, True)


    def kv_sum(h):
        kv.s[h] = tn(k[:, head(h)], v[:, head(h)]).astype(BF)

    for i, pair in enumerate(block_loads):
        pair[0].wait()
        pair[1].wait()
        loop(4 * i, 4 * i + 4, kv_sum)
    pl.semaphore_wait(barrier, 19)
    kv.send_core()
    cot_copies[0].start()
    near_cot.start()

    loads[0].wait()
    row = lax.broadcasted_iota(jnp.int32, (256, 256), 0)
    col = lax.broadcasted_iota(jnp.int32, (256, 256), 1)

    def lower(x):
        return jnp.where(row >= col, x, 0.0).astype(BF)

    def upper(x):
        return jnp.where(row <= col, x, 0.0).astype(BF)

    top, low = pl.ds(0, 256), pl.ds(256, 256)

    def causal(a, b, c, h):
        hs = head(h)
        a0, a1, b0, b1, c0, c1 = a[top, hs], a[low, hs], b[top, hs], b[low, hs], c[top, hs], c[low, hs]
        first = nn(lower(nt(a0, b0)), c0)
        second = nn(nt(a1, b0).astype(BF), c0) + nn(lower(nt(a1, b1)), c1)
        return first, second

    def scored(h):
        first, second = causal(q, k, v, h)
        intra[h, top] = first
        intra[h, low] = second

    def turned(h):
        hs = head(h)
        k0, k1, q0, q1 = k[top, hs], k[low, hs], q[top, hs], q[low, hs]
        sup[h, 0] = upper(nt(k0, q0))
        sup[h, 1] = nt(k0, q1).astype(BF)
        sup[h, 2] = upper(nt(k1, q1))

    loop(0, 4, scored)
    kv.send_x()
    cot_copies[1].start()
    cot_copies[2].start()
    loop(4, 16, scored)
    kv.send_up()

    for load in loads[1:4]:
        load.wait()

    def wrows(n):
        return pl.ds(pl.multiple_of(n * 256, 256), 256)

    def grad_own(n):
        gacc[:, wrows(n)] = nt(cot[tp], w[tp, wrows(n), :])

    each(0, 8, grad_own)
    loop(0, 8, turned)
    kv.send_down()

    def grad_top(n):
        g[top, wrows(n)] = (gacc[top, wrows(n)] + nt(cot[1 - tp, top, :], w[1 - tp, wrows(n), :])).astype(BF)

    def grad_low(n):
        g[low, wrows(n)] = (gacc[low, wrows(n)] + nt(cot[1 - tp, low, :], w[1 - tp, wrows(n), :])).astype(BF)

    loads[4].wait()
    loop(8, 16, turned)
    cot_copies[0].wait()
    cot_copies[1].wait()
    each(0, 8, grad_top)
    kv.send_back_x(mem)
    cot_copies[3].start()

    def top_rows(h):
        hs = head(h)
        g0 = g[top, hs]
        qacc[h] = tn(q[top, hs], g0)
        gacc[top, hs] = nn(sup[h, 0], g0)
        sup[h, 0] = upper(nt(v[top, hs], g0))

    loop(0, 16, top_rows)
    kv.send_back_core()
    kv.finish()

    def attend(h):
        a = intra[h] + nn(q[:, head(h)], kv.st[h])
        att[0, h // 4, h % 4] = a.T.astype(BF)

    att_copies = []
    for i in range(4):
        loop(4 * i, 4 * i + 4, attend)
        att_copies.append(remote(att.at[0, i], att.at[1, i], at_sem.at[0, i], at_sem.at[1, i], peer_core))
        att_copies[i].start()

    def query_top(h):
        hs = head(h)
        g0 = g[top, hs]
        qg[top, hs] = (nn(lower(nt(g0, v[top, hs])), k[top, hs]) + nt(g0, kv.st[h])).astype(BF)

    def query_low(h):
        hs = head(h)
        g1 = g[low, hs]
        r = nn(nt(g1, v[top, hs]).astype(BF), k[top, hs]) + nn(lower(nt(g1, v[low, hs])), k[low, hs])
        qg[low, hs] = (r + nt(g1, kv.st[h])).astype(BF)

    loop(0, 16, query_top)
    near_cot.wait()
    for copy in att_copies:
        copy.wait()

    y, z = at.y, at.z
    rings = []
    for i in range(4):
        pos, device = (y, at.along_y) if i % 2 == 0 else (z, at.along_z)
        rings.append(Ring(parts[i], lands[i], ring_sem.at[i], pos, device))
    ring_y, ring_z = rings[0], rings[1]
    last_z = Ring(s1a, land_a2, ring_sem.at[4], z, at.along_z)
    last_y = Ring(s1b, land_b2, ring_sem.at[5], y, at.along_y)

    def part(r, i):
        n = rings[r].quarters[i]
        cols = pl.ds(pl.multiple_of(core * 512 + 256 * (r % 2), 256), 256)
        near = cot[tp, :, cols] if r < 2 else cot[1 - tp, :, cols]
        far = pcot[r // 2, :, pl.ds(256 * (r % 2), 256)]
        ours = att[0, :, n] if r % 2 == 0 else att[0, n]
        theirs = att[1, :, n] if r % 2 == 0 else att[1, n]
        total = nn(ours.reshape(512, 512), near) + nn(theirs.reshape(512, 512), far)
        parts[r][n] = total.astype(BF).reshape(2, 2, 128, 256)

    for r in range(2):
        part(r, 2)
        rings[r].send_far()
    for r in range(2):
        part(r, 1)
        rings[r].send_near(0)
    cot_copies[2].wait()
    cot_copies[3].wait()
    far_cot.start()
    each(0, 8, grad_low)

    def qd_sum(h):
        qd.s[h] = (qacc[h] + tn(q[low, head(h)], g[low, head(h)])).astype(BF)

    loop(0, 16, qd_sum)
    qd.send_core()
    for r in range(2):
        part(r, 3)
        rings[r].send_near(1)
    qd.send_x()
    far_cot.wait()
    for r in range(2, 4):
        part(r, 2)
        rings[r].send_far()
    for r in range(2):
        rings[r].relay(0)
        rings[r].relay(1)
        part(r, 0)
    for r in range(2, 4):
        for i in (1, 3):
            part(r, i)
    qd.send_up()
    for r in range(2, 4):
        rings[r].send_near(0)
        rings[r].send_near(1)
    for r in range(2, 4):
        part(r, 0)

    def key_scored(h):
        hs = head(h)
        v0, v1, g1, q1 = v[top, hs], v[low, hs], g[low, hs], q[low, hs]
        intra[h, top] = nn(sup[h, 0], q[top, hs]) + nn(nt(v0, g1).astype(BF), q1)
        intra[h, low] = nn(upper(nt(v1, g1)), q1)

    def value_scored(h):
        g1 = g[low, head(h)]
        gacc[top, head(h)] += nn(sup[h, 1], g1)
        gacc[low, head(h)] = nn(sup[h, 2], g1)

    loop(0, 8, query_low)
    for r in range(2, 4):
        rings[r].relay(0)
        rings[r].relay(1)
    loop(8, 16, query_low)
    qd.send_down()

    def stage_two(firsts, second, to):
        for n, first in enumerate(firsts):
            first.wait_results()
            for half in range(2):
                part = first.result(half)
                for i in range(2):
                    to[2 * half + i, :, :, pl.ds(256 * n, 256)] = part[i].astype(BF).reshape(2, 64, 256)
        second.send_far()
        second.send_near(0)
        second.send_near(1)

    loop(0, 8, key_scored)
    loop(8, 12, key_scored)
    stage_two((rings[0], rings[2]), last_z, s1a)
    stage_two((rings[1], rings[3]), last_y, s1b)
    qd.send_back_x(None)
    loop(12, 16, key_scored)
    loop(0, 8, value_scored)
    last_z.relay(0)
    last_z.relay(1)
    last_y.relay(0)
    last_y.relay(1)
    loop(8, 16, value_scored)
    qd.send_back_core()

    def key_grad(h):
        hs = head(h)
        kg[:, hs] = (intra[h] + nt(v[:, hs], qd.st[h])).astype(BF)

    def value_grad(h):
        hs = head(h)
        vg[:, hs] = (gacc[:, hs] + nn(k[:, hs], qd.st[h])).astype(BF)

    def last(n, i):
        r = (at.p + i) % 4
        return remote(
            fin.at[n, r], fin_land.at[n, at.p], fin_sem.at[0, n, i - 1], fin_sem.at[1, n, i - 1], at.group(r)
        )

    def send_last(n, ring):
        ring.wait_results()
        for half in range(2):
            part = ring.result(half).astype(BF)
            for j in range(2):
                fin[n, half * 2 + j] = part[32 * j : 32 * j + 32]
        for i in range(1, 4):
            last(n, i).start()
        fin_land[n, at.p] = fin[n, at.p]

    send_last(0, last_z)
    loop(0, 8, lambda i: key_grad(8 * core + i))
    send_last(1, last_y)
    loop(0, 8, lambda i: value_grad(8 * core + i))
    qd.finish()
    loop(0, 8, lambda i: key_grad(8 * (1 - core) + i))
    loop(0, 8, lambda i: value_grad(8 * (1 - core) + i))
    for n in range(2):
        for i in range(1, 4):
            last(n, i).wait()
    for c in range(2):
        for n in range(2):
            total = fin_land[n, c].astype(F32) + fin_land[n, 2 + c].astype(F32)
            for i in range(2):
                start = (tp if i == 0 else 1 - tp) * 1024 + c * 512 + 256 * n
                wg[:, pl.ds(pl.multiple_of(start, 256), 256)] = total[:, 256 * i : 256 * i + 256]


def scan_scratch(kind):
    piece = VM((16, 32, 128), kind)
    return (
        VM((16, 128, 128), BF),
        VM((8, 128, 128), BF),
        VM((2, 4, 128, 128), BF),
        VM((4, 128, 128), BF),
        piece, piece, piece, piece,
        VM((4, 128, 128), F32),
        VM((4, 128, 128), BF),
        VM((4, 128, 128), BF),
        VM((8, 128, 128), BF),
        VM((16, 128, 128), BF),
        DMA((2, 4)),
        DMA((2,)),
        DMA((2,)),
    )


def put_out(*refs):
    sems = refs[8]
    copies = [pltpu.make_async_copy(refs[i], refs[4 + i], sems.at[i]) for i in range(4)]
    for copy in copies:
        copy.start()
    for copy in copies:
        copy.wait()


def local(queries, keys, values, cotangent, out_weight, memory):
    tok = VM((512, 2048), BF)
    any_spec = pl.BlockSpec(memory_space=pl.ANY)
    like = jax.ShapeDtypeStruct((512, 2048), BF)
    grads = pl.pallas_call(
        kernel,
        out_shape=(VM((512, 2048), BF), VM((512, 2048), BF), VM((512, 2048), BF), VM((32, 2048), F32)),
        in_specs=[any_spec] * 6,
        out_specs=(pl.BlockSpec(memory_space=VM),) * 4,
        scratch_shapes=[
            tok, tok, tok,
            VM((2, 2048, 1024), BF),
            VM((2, 512, 1024), BF),
            VM((2, 512, 512), BF),
            VM((4, 128, 128), F32),
            VM((512, 2048), F32),
            tok,
            VM((16, 512, 128), F32),
            scan_scratch(F32),
            scan_scratch(BF),
            VM((16, 3, 256, 256), BF),
            VM((16, 128, 128), F32),
            VM((2, 4, 4, 128, 512), BF),
            (VM((4, 2, 2, 128, 256), BF),) * 4,
            (VM((2, 3, 2, 128, 256), BF),) * 4,
            VM((4, 2, 64, 512), BF),
            VM((4, 2, 64, 512), BF),
            VM((2, 3, 64, 512), BF),
            VM((2, 3, 64, 512), BF),
            VM((2, 4, 32, 512), BF),
            VM((2, 4, 32, 512), BF),
            DMA((15,)),
            DMA((2, 4)),
            DMA((2, 2)),
            DMA((2, 4)),
            DMA((6, 2, 2, 3)),
            DMA((2, 2, 3)),
        ],
        compiler_params=pltpu.CompilerParams(
            collective_id=0, has_side_effects=True, vmem_limit_bytes=59768832
        ),
    )(queries, keys, values, cotangent, out_weight, memory)
    return pl.pallas_call(
        put_out,
        out_shape=(like, like, like, jax.ShapeDtypeStruct((32, 2048), F32)),
        in_specs=[any_spec] * 4,
        out_specs=(any_spec,) * 4,
        scratch_shapes=[DMA((4,))],
        compiler_params=pltpu.CompilerParams(vmem_limit_bytes=1048576),
    )(*grads)


def solution(mesh):
    in_specs = (
        P("ctx", "tp"),
        P("ctx", "tp"),
        P("ctx", "tp"),
        P("ctx", "tp"),
        P("tp", None),
        P("tp", None, None),
    )
    out_specs = (P("ctx", "tp"), P("ctx", "tp"), P("ctx", "tp"), P(("tp", "ctx"), None))
    return jax.shard_map(local, mesh=mesh, in_specs=in_specs, out_specs=out_specs, check_vma=False)
```

```python
import jax
import jax.numpy as jnp
from jax import lax
from jax.experimental import pallas as pl
from jax.experimental.pallas import tpu as pltpu
from jax.sharding import PartitionSpec as P

MESH = pl.DeviceIdType.MESH
BF = jnp.bfloat16
F32 = jnp.float32
VM = pltpu.VMEM
DMA = pltpu.SemaphoreType.DMA


def nn(a, b):
    return lax.dot_general(a, b, (((1,), (0,)), ((), ())), preferred_element_type=F32)


def nt(a, b):
    return lax.dot_general(a, b, (((1,), (1,)), ((), ())), preferred_element_type=F32)


def tn(a, b):
    return lax.dot_general(a, b, (((0,), (0,)), ((), ())), preferred_element_type=F32)


def head(h):
    return pl.ds(pl.multiple_of(h * 128, 128), 128)


def loop(lo, hi, body):
    side = 4 if (hi - lo) % 4 == 0 else 2

    def step(i, carry):
        for j in range(side):
            body(lo + side * i + j)
        return carry

    lax.fori_loop(0, (hi - lo) // side, step, 0)


def each(lo, hi, body):
    def step(i, carry):
        body(i)
        return carry

    lax.fori_loop(lo, hi, step, 0)


class Place:
    def __init__(self):
        self.me = lax.axis_index("ctx")
        self.tp = lax.axis_index("tp")
        self.p = self.me % 4
        self.core = self.me % 2
        self.x = self.p // 2
        self.zy = self.me // 4
        self.z = self.me // 16
        self.y = self.zy % 4
        self.base = self.me - self.p

    def other_core(self):
        return (self.base + 2 * self.x + 1 - self.core, self.tp)

    def other_x(self):
        return (self.base + 2 * (1 - self.x) + self.core, self.tp)

    def group(self, p):
        return (self.base + p, self.tp)

    def plane(self, zy):
        return (zy * 4 + self.p, self.tp)

    def along_y(self, y):
        return (self.me + (y - self.y) * 4, self.tp)

    def along_z(self, z):
        return (self.me + (z - self.z) * 16, self.tp)


def remote(src, dst, send, recv, device):
    return pltpu.make_async_remote_copy(
        src_ref=src, dst_ref=dst, send_sem=send, recv_sem=recv, device_id=device, device_id_type=MESH
    )


class Scan:
    def __init__(self, at, refs, reverse):
        self.at, self.reverse = at, reverse
        (self.s, self.a, self.pc, self.px, self.t, self.b, self.pre, self.c, self.run, self.e, self.f, self.d, self.st,
         self.sem, self.up, self.down) = refs
        self.copies = [
            remote(self.s.at[pl.ds(8 * (1 - at.core), 8)], self.a, self.sem.at[0, 0], self.sem.at[1, 0], at.other_core()),
            remote(self.pc.at[1 - at.x], self.px, self.sem.at[0, 1], self.sem.at[1, 1], at.other_x()),
            remote(self.e, self.f, self.sem.at[0, 2], self.sem.at[1, 2], at.other_x()),
            remote(self.d, self.st.at[pl.ds(8 * at.core, 8)], self.sem.at[0, 3], self.sem.at[1, 3], at.other_core()),
        ]

    def send_core(self):
        self.copies[0].start()

    def send_x(self):
        self.copies[0].wait()
        for i in range(2):
            for h in range(4):
                own = self.s[8 * self.at.core + 4 * i + h].astype(F32)
                self.pc[i, h] = (own + self.a[4 * i + h].astype(F32)).astype(BF)
        self.copies[1].start()

    def up_plane(self, k):
        j = (self.at.zy + k) % 16
        return remote(self.t.at[j], self.b.at[self.at.zy], self.up.at[0], self.up.at[1], self.at.plane(j))

    def send_up(self):
        self.copies[1].wait()
        for h in range(4):
            total = self.pc[self.at.x, h].astype(F32) + self.px[h].astype(F32)
            self.t[pl.ds(4 * h, 4)] = total.reshape(4, 32, 128).astype(self.t.dtype)
        each(1, 16, lambda k: self.up_plane(k).start())
        self.b[self.at.zy] = self.t[self.at.zy]

    def down_plane(self, k):
        j = (self.at.zy + k) % 16
        return remote(self.pre.at[j], self.c.at[self.at.zy], self.down.at[0], self.down.at[1], self.at.plane(j))

    def wait_all(self, src, dst, sems):
        pltpu.make_async_copy(src.at[pl.ds(0, 15)], src.at[pl.ds(0, 15)], sems.at[0]).wait()
        pltpu.make_async_copy(dst.at[pl.ds(0, 15)], dst.at[pl.ds(0, 15)], sems.at[1]).wait()

    def send_down(self):
        self.wait_all(self.t, self.b, self.up)
        run = jnp.zeros((32, 128), F32)
        for i in reversed(range(16)) if self.reverse else range(16):
            self.pre[i] = run.astype(self.pre.dtype)
            run = run + self.b[i].astype(F32)
        each(1, 16, lambda k: self.down_plane(k).start())
        self.c[self.at.zy] = self.pre[self.at.zy]

    def send_back_x(self, memory):
        self.wait_all(self.pre, self.c, self.down)
        after = self.at.x == (0 if self.reverse else 1)
        for h in range(4):
            run = self.c[pl.ds(4 * h, 4)].astype(F32).reshape(128, 128)
            if memory is not None:
                run = run + memory[h]
            mine, theirs = self.pc[self.at.x, h].astype(F32), self.px[h].astype(F32)
            self.e[h] = (run + jnp.where(after, 0.0, mine)).astype(BF)
            self.run[h] = run + jnp.where(after, theirs, 0.0)
        self.copies[2].start()

    def send_back_core(self):
        self.copies[2].wait()
        after = self.at.core == (0 if self.reverse else 1)
        first = 8 * self.at.core

        def settle(run, h):
            mine, theirs = self.s[first + h].astype(F32), self.a[h].astype(F32)
            self.d[h] = (run + jnp.where(after, 0.0, mine)).astype(BF)
            self.st[first + h] = (run + jnp.where(after, theirs, 0.0)).astype(BF)

        for h in range(4):
            settle(self.run[h], 4 * self.at.x + h)
            settle(self.f[h].astype(F32), 4 * (1 - self.at.x) + h)
        self.copies[3].start()

    def finish(self):
        self.copies[3].wait()


class Ring:
    def __init__(self, src, land, sems, pos, device):
        self.src, self.land, self.sems, self.pos = src, land, sems, pos
        self.quarters = [pos, (pos + 1) % 4, (pos + 2) % 4, (pos + 3) % 4]
        self.device = device

    def copy(self, way, slot):
        near = self.quarters[1] if way == 0 else self.quarters[3]
        if slot == 0:
            src = self.src.at[self.quarters[2], way]
        elif slot == 1:
            src = self.src.at[near, 1 - way]
        else:
            src = self.src.at[near, way]
        return remote(
            src, self.land.at[way, slot], self.sems.at[0, way, slot], self.sems.at[1, way, slot], self.device(near)
        )

    def send_far(self):
        self.copy(0, 0).start()
        self.copy(1, 0).start()

    def send_near(self, way):
        self.copy(way, 1).start()

    def relay(self, way):
        near = self.quarters[1] if way == 0 else self.quarters[3]
        self.copy(way, 0).wait()
        self.src[near, way] = (self.src[near, way].astype(F32) + self.land[way, 0].astype(F32)).astype(BF)
        self.copy(way, 2).start()

    def result(self, half):
        own = self.src[self.pos, half].astype(F32)
        for way in range(2):
            slot = 2 if way == half else 1
            own = own + self.land[way, slot].astype(F32)
        return own

    def wait_results(self):
        for way in range(2):
            self.copy(way, 1).wait()
            self.copy(way, 2).wait()


def kernel(
    q_hbm, k_hbm, v_hbm, cot_hbm, w_hbm, mem_hbm,
    qg, kg, vg, wg,
    q, k, v, w, cot, pcot, mem, gacc, g, intra,
    kv_refs, qd_refs,
    sup, qacc, att, parts, lands, s1a, s1b, land_a2, land_b2, fin, fin_land,
    in_sem, tp_sem, pc_sem, at_sem, ring_sem, fin_sem,
):
    at = Place()
    me, tp, core = at.me, at.tp, at.core
    peer_core = at.other_core()
    peer_tp = (me, 1 - tp)

    loads = [
        pltpu.make_async_copy(q_hbm, q, in_sem.at[2]),
        pltpu.make_async_copy(cot_hbm, cot.at[tp], in_sem.at[3]),
        pltpu.make_async_copy(w_hbm.at[:, pl.ds(0, 1024)], w.at[0], in_sem.at[4]),
        pltpu.make_async_copy(w_hbm.at[:, pl.ds(1024, 1024)], w.at[1], in_sem.at[5]),
        pltpu.make_async_copy(mem_hbm.at[pl.ds(8 * core + 4 * at.x, 4)], mem, in_sem.at[6]),
    ]
    def block(src, dst, i, sem):
        return pltpu.make_async_copy(src.at[:, pl.ds(512 * i, 512)], dst.at[:, pl.ds(512 * i, 512)], in_sem.at[sem])

    block_loads = [(block(k_hbm, k, i, 7 + i), block(v_hbm, v, i, 11 + i)) for i in range(4)]
    for pair in block_loads:
        pair[0].start()
        pair[1].start()
    for load in loads:
        load.start()

    barrier = pltpu.get_barrier_semaphore()

    def signal(device):
        pl.semaphore_signal(barrier, inc=1, device_id=device, device_id_type=MESH)

    signal(peer_tp)
    for i in range(1, 4):
        signal(at.group((at.p + i) % 4))
    each(1, 16, lambda i: signal(at.plane((at.zy + i) % 16)))

    def mine(c):
        return pl.ds(pl.multiple_of(c * 512, 512), 512)

    cot_copies = [
        remote(cot_hbm.at[rows], cot.at[tp, rows], tp_sem.at[0, i], tp_sem.at[1, i], peer_tp)
        for i, rows in enumerate((pl.ds(0, 64), pl.ds(64, 192), pl.ds(256, 64), pl.ds(320, 96), pl.ds(416, 96)))
    ]
    near_cot = remote(cot_hbm.at[:, mine(1 - core)], pcot.at[0], pc_sem.at[0, 0], pc_sem.at[1, 0], peer_core)
    far_cot = remote(cot.at[1 - tp, :, mine(1 - core)], pcot.at[1], pc_sem.at[0, 1], pc_sem.at[1, 1], peer_core)

    kv = Scan(at, kv_refs, False)
    qd = Scan(at, qd_refs, True)


    def kv_sum(h):
        kv.s[h] = tn(k[:, head(h)], v[:, head(h)]).astype(BF)

    for i, pair in enumerate(block_loads):
        pair[0].wait()
        pair[1].wait()
        loop(4 * i, 4 * i + 4, kv_sum)
    pl.semaphore_wait(barrier, 19)
    kv.send_core()
    cot_copies[0].start()
    near_cot.start()

    loads[0].wait()
    row = lax.broadcasted_iota(jnp.int32, (256, 256), 0)
    col = lax.broadcasted_iota(jnp.int32, (256, 256), 1)

    def lower(x):
        return jnp.where(row >= col, x, 0.0).astype(BF)

    def upper(x):
        return jnp.where(row <= col, x, 0.0).astype(BF)

    top, low = pl.ds(0, 256), pl.ds(256, 256)

    def causal(a, b, c, h):
        hs = head(h)
        a0, a1, b0, b1, c0, c1 = a[top, hs], a[low, hs], b[top, hs], b[low, hs], c[top, hs], c[low, hs]
        first = nn(lower(nt(a0, b0)), c0)
        second = nn(nt(a1, b0).astype(BF), c0) + nn(lower(nt(a1, b1)), c1)
        return first, second

    def scored(h):
        first, second = causal(q, k, v, h)
        intra[h, top] = first
        intra[h, low] = second

    def turned(h):
        hs = head(h)
        k0, k1, q0, q1 = k[top, hs], k[low, hs], q[top, hs], q[low, hs]
        sup[h, 0] = upper(nt(k0, q0))
        sup[h, 1] = nt(k0, q1).astype(BF)
        sup[h, 2] = upper(nt(k1, q1))

    loop(0, 4, scored)
    kv.send_x()
    cot_copies[1].start()
    cot_copies[2].start()
    loop(4, 16, scored)
    kv.send_up()

    for load in loads[1:4]:
        load.wait()

    def wrows(n):
        return pl.ds(pl.multiple_of(n * 256, 256), 256)

    def grad_own(n):
        gacc[:, wrows(n)] = nt(cot[tp], w[tp, wrows(n), :])

    each(0, 8, grad_own)
    loop(0, 4, turned)
    kv.send_down()
    loop(4, 16, turned)

    def grad_top(n):
        g[top, wrows(n)] = (gacc[top, wrows(n)] + nt(cot[1 - tp, top, :], w[1 - tp, wrows(n), :])).astype(BF)

    def grad_low(n):
        g[low, wrows(n)] = (gacc[low, wrows(n)] + nt(cot[1 - tp, low, :], w[1 - tp, wrows(n), :])).astype(BF)

    loads[4].wait()
    cot_copies[0].wait()
    cot_copies[1].wait()
    each(0, 4, grad_top)
    kv.send_back_x(mem)
    cot_copies[3].start()
    each(4, 8, grad_top)

    def top_rows(h):
        hs = head(h)
        g0 = g[top, hs]
        qacc[h] = tn(q[top, hs], g0)
        gacc[top, hs] = nn(sup[h, 0], g0)
        sup[h, 0] = upper(nt(v[top, hs], g0))

    loop(0, 16, top_rows)
    kv.send_back_core()
    cot_copies[4].start()
    kv.finish()

    def attend(h):
        a = intra[h] + nn(q[:, head(h)], kv.st[h])
        att[0, h // 4, h % 4] = a.T.astype(BF)

    att_copies = []
    for i in range(4):
        loop(4 * i, 4 * i + 4, attend)
        att_copies.append(remote(att.at[0, i], att.at[1, i], at_sem.at[0, i], at_sem.at[1, i], peer_core))
        att_copies[i].start()

    def query_top(h):
        hs = head(h)
        g0 = g[top, hs]
        qg[top, hs] = (nn(lower(nt(g0, v[top, hs])), k[top, hs]) + nt(g0, kv.st[h])).astype(BF)

    def query_low(h):
        hs = head(h)
        g1 = g[low, hs]
        r = nn(nt(g1, v[top, hs]).astype(BF), k[top, hs]) + nn(lower(nt(g1, v[low, hs])), k[low, hs])
        qg[low, hs] = (r + nt(g1, kv.st[h])).astype(BF)

    loop(0, 16, query_top)
    near_cot.wait()
    for copy in att_copies:
        copy.wait()

    y, z = at.y, at.z
    rings = []
    for i in range(4):
        pos, device = (y, at.along_y) if i % 2 == 0 else (z, at.along_z)
        rings.append(Ring(parts[i], lands[i], ring_sem.at[i], pos, device))
    ring_y, ring_z = rings[0], rings[1]
    last_z = Ring(s1a, land_a2, ring_sem.at[4], z, at.along_z)
    last_y = Ring(s1b, land_b2, ring_sem.at[5], y, at.along_y)

    def part(r, i):
        n = rings[r].quarters[i]
        cols = pl.ds(pl.multiple_of(core * 512 + 256 * (r % 2), 256), 256)
        near = cot[tp, :, cols] if r < 2 else cot[1 - tp, :, cols]
        far = pcot[r // 2, :, pl.ds(256 * (r % 2), 256)]
        ours = att[0, :, n] if r % 2 == 0 else att[0, n]
        theirs = att[1, :, n] if r % 2 == 0 else att[1, n]
        total = nn(ours.reshape(512, 512), near) + nn(theirs.reshape(512, 512), far)
        parts[r][n] = total.astype(BF).reshape(2, 2, 128, 256)

    for r in range(2):
        part(r, 2)
        rings[r].send_far()
    for r in range(2):
        for way, i in ((0, 1), (1, 3)):
            part(r, i)
            rings[r].send_near(way)
    for copy in cot_copies[2:]:
        copy.wait()
    far_cot.start()
    each(0, 8, grad_low)
    for r in range(2):
        rings[r].relay(0)
        rings[r].relay(1)

    def qd_sum(h):
        qd.s[h] = (qacc[h] + tn(q[low, head(h)], g[low, head(h)])).astype(BF)

    loop(0, 16, qd_sum)
    qd.send_core()
    far_cot.wait()
    for r in range(2, 4):
        part(r, 2)
        rings[r].send_far()
    part(2, 1)
    rings[2].send_near(0)
    qd.send_x()
    for r, way, i in ((2, 1, 3), (3, 0, 1), (3, 1, 3)):
        part(r, i)
        rings[r].send_near(way)
    for r in range(4):
        part(r, 0)
    loop(0, 8, query_low)
    qd.send_up()
    for r in range(2, 4):
        rings[r].relay(0)
        rings[r].relay(1)
    loop(8, 16, query_low)

    def key_scored(h):
        hs = head(h)
        v0, v1, g1, q1 = v[top, hs], v[low, hs], g[low, hs], q[low, hs]
        intra[h, top] = nn(sup[h, 0], q[top, hs]) + nn(nt(v0, g1).astype(BF), q1)
        intra[h, low] = nn(upper(nt(v1, g1)), q1)

    def value_scored(h):
        g1 = g[low, head(h)]
        gacc[top, head(h)] += nn(sup[h, 1], g1)
        gacc[low, head(h)] = nn(sup[h, 2], g1)

    def stage_two(firsts, second, to):
        for n, first in enumerate(firsts):
            first.wait_results()
            for half in range(2):
                part = first.result(half)
                for i in range(2):
                    to[2 * half + i, :, :, pl.ds(256 * n, 256)] = part[i].astype(BF).reshape(2, 64, 256)
        second.send_far()
        second.send_near(0)
        second.send_near(1)

    loop(0, 4, key_scored)
    qd.send_down()
    loop(4, 8, key_scored)
    stage_two((rings[0], rings[2]), last_z, s1a)
    stage_two((rings[1], rings[3]), last_y, s1b)
    loop(8, 16, key_scored)
    loop(0, 8, value_scored)
    qd.send_back_x(None)
    last_z.relay(0)
    last_z.relay(1)
    last_y.relay(0)
    last_y.relay(1)
    loop(8, 16, value_scored)

    def key_grad(h):
        hs = head(h)
        kg[:, hs] = (intra[h] + nt(v[:, hs], qd.st[h])).astype(BF)

    def value_grad(h):
        hs = head(h)
        vg[:, hs] = (gacc[:, hs] + nn(k[:, hs], qd.st[h])).astype(BF)

    def last(n, i):
        r = (at.p + i) % 4
        return remote(
            fin.at[n, r], fin_land.at[n, at.p], fin_sem.at[0, n, i - 1], fin_sem.at[1, n, i - 1], at.group(r)
        )

    def send_last(n, ring):
        ring.wait_results()
        for half in range(2):
            part = ring.result(half).astype(BF)
            for j in range(2):
                fin[n, half * 2 + j] = part[32 * j : 32 * j + 32]
        for i in range(1, 4):
            last(n, i).start()
        fin_land[n, at.p] = fin[n, at.p]

    send_last(0, last_z)
    send_last(1, last_y)
    qd.send_back_core()
    loop(0, 8, lambda i: key_grad(8 * core + i))
    loop(0, 8, lambda i: value_grad(8 * core + i))
    qd.finish()
    loop(0, 8, lambda i: key_grad(8 * (1 - core) + i))
    loop(0, 8, lambda i: value_grad(8 * (1 - core) + i))
    for n in range(2):
        for i in range(1, 4):
            last(n, i).wait()
    for c in range(2):
        for n in range(2):
            total = fin_land[n, c].astype(F32) + fin_land[n, 2 + c].astype(F32)
            for i in range(2):
                start = (tp if i == 0 else 1 - tp) * 1024 + c * 512 + 256 * n
                wg[:, pl.ds(pl.multiple_of(start, 256), 256)] = total[:, 256 * i : 256 * i + 256]


def scan_scratch(kind):
    piece = VM((16, 32, 128), kind)
    return (
        VM((16, 128, 128), BF),
        VM((8, 128, 128), BF),
        VM((2, 4, 128, 128), BF),
        VM((4, 128, 128), BF),
        piece, piece, piece, piece,
        VM((4, 128, 128), F32),
        VM((4, 128, 128), BF),
        VM((4, 128, 128), BF),
        VM((8, 128, 128), BF),
        VM((16, 128, 128), BF),
        DMA((2, 4)),
        DMA((2,)),
        DMA((2,)),
    )


def put_out(*refs):
    sems = refs[8]
    copies = [pltpu.make_async_copy(refs[i], refs[4 + i], sems.at[i]) for i in range(4)]
    for copy in copies:
        copy.start()
    for copy in copies:
        copy.wait()


def local(queries, keys, values, cotangent, out_weight, memory):
    tok = VM((512, 2048), BF)
    any_spec = pl.BlockSpec(memory_space=pl.ANY)
    like = jax.ShapeDtypeStruct((512, 2048), BF)
    grads = pl.pallas_call(
        kernel,
        out_shape=(VM((512, 2048), BF), VM((512, 2048), BF), VM((512, 2048), BF), VM((32, 2048), F32)),
        in_specs=[any_spec] * 6,
        out_specs=(pl.BlockSpec(memory_space=VM),) * 4,
        scratch_shapes=[
            tok, tok, tok,
            VM((2, 2048, 1024), BF),
            VM((2, 512, 1024), BF),
            VM((2, 512, 512), BF),
            VM((4, 128, 128), F32),
            VM((512, 2048), F32),
            tok,
            VM((16, 512, 128), F32),
            scan_scratch(F32),
            scan_scratch(BF),
            VM((16, 3, 256, 256), BF),
            VM((16, 128, 128), F32),
            VM((2, 4, 4, 128, 512), BF),
            (VM((4, 2, 2, 128, 256), BF),) * 4,
            (VM((2, 3, 2, 128, 256), BF),) * 4,
            VM((4, 2, 64, 512), BF),
            VM((4, 2, 64, 512), BF),
            VM((2, 3, 64, 512), BF),
            VM((2, 3, 64, 512), BF),
            VM((2, 4, 32, 512), BF),
            VM((2, 4, 32, 512), BF),
            DMA((15,)),
            DMA((2, 5)),
            DMA((2, 2)),
            DMA((2, 4)),
            DMA((6, 2, 2, 3)),
            DMA((2, 2, 3)),
        ],
        compiler_params=pltpu.CompilerParams(
            collective_id=0, has_side_effects=True, vmem_limit_bytes=59768832
        ),
    )(queries, keys, values, cotangent, out_weight, memory)
    return pl.pallas_call(
        put_out,
        out_shape=(like, like, like, jax.ShapeDtypeStruct((32, 2048), F32)),
        in_specs=[any_spec] * 4,
        out_specs=(any_spec,) * 4,
        scratch_shapes=[DMA((4,))],
        compiler_params=pltpu.CompilerParams(vmem_limit_bytes=1048576),
    )(*grads)


def solution(mesh):
    in_specs = (
        P("ctx", "tp"),
        P("ctx", "tp"),
        P("ctx", "tp"),
        P("ctx", "tp"),
        P("tp", None),
        P("tp", None, None),
    )
    out_specs = (P("ctx", "tp"), P("ctx", "tp"), P("ctx", "tp"), P(("tp", "ctx"), None))
    return jax.shard_map(local, mesh=mesh, in_specs=in_specs, out_specs=out_specs, check_vma=False)
```

```python
import jax
import jax.numpy as jnp
from jax import lax
from jax.experimental import pallas as pl
from jax.experimental.pallas import tpu as pltpu
from jax.sharding import PartitionSpec as P

MESH = pl.DeviceIdType.MESH
BF = jnp.bfloat16
F32 = jnp.float32
VM = pltpu.VMEM
DMA = pltpu.SemaphoreType.DMA


def nn(a, b):
    return lax.dot_general(a, b, (((1,), (0,)), ((), ())), preferred_element_type=F32)


def nt(a, b):
    return lax.dot_general(a, b, (((1,), (1,)), ((), ())), preferred_element_type=F32)


def tn(a, b):
    return lax.dot_general(a, b, (((0,), (0,)), ((), ())), preferred_element_type=F32)


def head(h):
    return pl.ds(pl.multiple_of(h * 128, 128), 128)


def loop(lo, hi, body):
    side = 4 if (hi - lo) % 4 == 0 else 2

    def step(i, carry):
        for j in range(side):
            body(lo + side * i + j)
        return carry

    lax.fori_loop(0, (hi - lo) // side, step, 0)


def each(lo, hi, body):
    def step(i, carry):
        body(i)
        return carry

    lax.fori_loop(lo, hi, step, 0)


class Place:
    def __init__(self):
        self.me = lax.axis_index("ctx")
        self.tp = lax.axis_index("tp")
        self.p = self.me % 4
        self.core = self.me % 2
        self.x = self.p // 2
        self.zy = self.me // 4
        self.z = self.me // 16
        self.y = self.zy % 4
        self.base = self.me - self.p

    def other_core(self):
        return (self.base + 2 * self.x + 1 - self.core, self.tp)

    def other_x(self):
        return (self.base + 2 * (1 - self.x) + self.core, self.tp)

    def group(self, p):
        return (self.base + p, self.tp)

    def plane(self, zy):
        return (zy * 4 + self.p, self.tp)

    def along_y(self, y):
        return (self.me + (y - self.y) * 4, self.tp)

    def along_z(self, z):
        return (self.me + (z - self.z) * 16, self.tp)


def remote(src, dst, send, recv, device):
    return pltpu.make_async_remote_copy(
        src_ref=src, dst_ref=dst, send_sem=send, recv_sem=recv, device_id=device, device_id_type=MESH
    )


class Scan:
    def __init__(self, at, refs, reverse):
        self.at, self.reverse = at, reverse
        (self.s, self.a, self.pc, self.px, self.t, self.b, self.pre, self.c, self.run, self.e, self.f, self.d, self.st,
         self.sem, self.up, self.down) = refs
        self.copies = [
            remote(self.s.at[pl.ds(8 * (1 - at.core), 8)], self.a, self.sem.at[0, 0], self.sem.at[1, 0], at.other_core()),
            remote(self.pc.at[1 - at.x], self.px, self.sem.at[0, 1], self.sem.at[1, 1], at.other_x()),
            remote(self.e, self.f, self.sem.at[0, 2], self.sem.at[1, 2], at.other_x()),
            remote(self.d, self.st.at[pl.ds(8 * at.core, 8)], self.sem.at[0, 3], self.sem.at[1, 3], at.other_core()),
        ]

    def send_core(self):
        self.copies[0].start()

    def send_x(self):
        self.copies[0].wait()
        for i in range(2):
            for h in range(4):
                own = self.s[8 * self.at.core + 4 * i + h].astype(F32)
                self.pc[i, h] = (own + self.a[4 * i + h].astype(F32)).astype(BF)
        self.copies[1].start()

    def up_plane(self, k):
        j = (self.at.zy + k) % 16
        return remote(self.t.at[j], self.b.at[self.at.zy], self.up.at[0], self.up.at[1], self.at.plane(j))

    def send_up(self):
        self.copies[1].wait()
        for h in range(4):
            total = self.pc[self.at.x, h].astype(F32) + self.px[h].astype(F32)
            self.t[pl.ds(4 * h, 4)] = total.reshape(4, 32, 128).astype(self.t.dtype)
        each(1, 16, lambda k: self.up_plane(k).start())
        self.b[self.at.zy] = self.t[self.at.zy]

    def down_plane(self, k):
        j = (self.at.zy + k) % 16
        return remote(self.pre.at[j], self.c.at[self.at.zy], self.down.at[0], self.down.at[1], self.at.plane(j))

    def wait_all(self, src, dst, sems):
        pltpu.make_async_copy(src.at[pl.ds(0, 15)], src.at[pl.ds(0, 15)], sems.at[0]).wait()
        pltpu.make_async_copy(dst.at[pl.ds(0, 15)], dst.at[pl.ds(0, 15)], sems.at[1]).wait()

    def send_down(self):
        self.wait_all(self.t, self.b, self.up)
        run = jnp.zeros((32, 128), F32)
        for i in reversed(range(16)) if self.reverse else range(16):
            self.pre[i] = run.astype(self.pre.dtype)
            run = run + self.b[i].astype(F32)
        each(1, 16, lambda k: self.down_plane(k).start())
        self.c[self.at.zy] = self.pre[self.at.zy]

    def send_back_x(self, memory):
        self.wait_all(self.pre, self.c, self.down)
        after = self.at.x == (0 if self.reverse else 1)
        for h in range(4):
            run = self.c[pl.ds(4 * h, 4)].astype(F32).reshape(128, 128)
            if memory is not None:
                run = run + memory[h]
            mine, theirs = self.pc[self.at.x, h].astype(F32), self.px[h].astype(F32)
            self.e[h] = (run + jnp.where(after, 0.0, mine)).astype(BF)
            self.run[h] = run + jnp.where(after, theirs, 0.0)
        self.copies[2].start()

    def send_back_core(self):
        self.copies[2].wait()
        after = self.at.core == (0 if self.reverse else 1)
        first = 8 * self.at.core

        def settle(run, h):
            mine, theirs = self.s[first + h].astype(F32), self.a[h].astype(F32)
            self.d[h] = (run + jnp.where(after, 0.0, mine)).astype(BF)
            self.st[first + h] = (run + jnp.where(after, theirs, 0.0)).astype(BF)

        for h in range(4):
            settle(self.run[h], 4 * self.at.x + h)
            settle(self.f[h].astype(F32), 4 * (1 - self.at.x) + h)
        self.copies[3].start()

    def finish(self):
        self.copies[3].wait()


class Ring:
    def __init__(self, src, land, sems, pos, device):
        self.src, self.land, self.sems, self.pos = src, land, sems, pos
        self.quarters = [pos, (pos + 1) % 4, (pos + 2) % 4, (pos + 3) % 4]
        self.device = device

    def copy(self, way, slot):
        near = self.quarters[1] if way == 0 else self.quarters[3]
        if slot == 0:
            src = self.src.at[self.quarters[2], way]
        elif slot == 1:
            src = self.src.at[near, 1 - way]
        else:
            src = self.src.at[near, way]
        return remote(
            src, self.land.at[way, slot], self.sems.at[0, way, slot], self.sems.at[1, way, slot], self.device(near)
        )

    def send_far(self):
        self.copy(0, 0).start()
        self.copy(1, 0).start()

    def send_near(self, way):
        self.copy(way, 1).start()

    def relay(self, way):
        near = self.quarters[1] if way == 0 else self.quarters[3]
        self.copy(way, 0).wait()
        self.src[near, way] = (self.src[near, way].astype(F32) + self.land[way, 0].astype(F32)).astype(BF)
        self.copy(way, 2).start()

    def result(self, half):
        own = self.src[self.pos, half].astype(F32)
        for way in range(2):
            slot = 2 if way == half else 1
            own = own + self.land[way, slot].astype(F32)
        return own

    def wait_results(self):
        for way in range(2):
            self.copy(way, 1).wait()
            self.copy(way, 2).wait()


def kernel(
    q_hbm, k_hbm, v_hbm, cot_hbm, w_hbm, mem_hbm,
    qg, kg, vg, wg,
    q, k, v, w, cot, pcot, mem, gacc, g, intra,
    kv_refs, qd_refs,
    sup, qacc, att, parts, lands, s1a, s1b, land_a2, land_b2, fin, fin_land,
    in_sem, tp_sem, pc_sem, at_sem, ring_sem, fin_sem,
):
    at = Place()
    me, tp, core = at.me, at.tp, at.core
    peer_core = at.other_core()
    peer_tp = (me, 1 - tp)

    loads = [
        pltpu.make_async_copy(q_hbm, q, in_sem.at[2]),
        pltpu.make_async_copy(cot_hbm, cot.at[tp], in_sem.at[3]),
        pltpu.make_async_copy(w_hbm.at[:, pl.ds(0, 1024)], w.at[0], in_sem.at[4]),
        pltpu.make_async_copy(w_hbm.at[:, pl.ds(1024, 1024)], w.at[1], in_sem.at[5]),
        pltpu.make_async_copy(mem_hbm.at[pl.ds(8 * core + 4 * at.x, 4)], mem, in_sem.at[6]),
    ]
    def block(src, dst, i, sem):
        return pltpu.make_async_copy(src.at[:, pl.ds(512 * i, 512)], dst.at[:, pl.ds(512 * i, 512)], in_sem.at[sem])

    block_loads = [(block(k_hbm, k, i, 7 + i), block(v_hbm, v, i, 11 + i)) for i in range(4)]
    for pair in block_loads:
        pair[0].start()
        pair[1].start()
    for load in loads:
        load.start()

    barrier = pltpu.get_barrier_semaphore()

    def signal(device):
        pl.semaphore_signal(barrier, inc=1, device_id=device, device_id_type=MESH)

    signal(peer_tp)
    for i in range(1, 4):
        signal(at.group((at.p + i) % 4))
    each(1, 16, lambda i: signal(at.plane((at.zy + i) % 16)))

    def mine(c):
        return pl.ds(pl.multiple_of(c * 512, 512), 512)

    cot_copies = [
        remote(cot_hbm.at[rows], cot.at[tp, rows], tp_sem.at[0, i], tp_sem.at[1, i], peer_tp)
        for i, rows in enumerate((pl.ds(0, 64), pl.ds(64, 192), pl.ds(256, 64), pl.ds(320, 96), pl.ds(416, 96)))
    ]
    near_cot = remote(cot_hbm.at[:, mine(1 - core)], pcot.at[0], pc_sem.at[0, 0], pc_sem.at[1, 0], peer_core)
    far_cot = remote(cot.at[1 - tp, :, mine(1 - core)], pcot.at[1], pc_sem.at[0, 1], pc_sem.at[1, 1], peer_core)

    kv = Scan(at, kv_refs, False)
    qd = Scan(at, qd_refs, True)


    def kv_sum(h):
        kv.s[h] = tn(k[:, head(h)], v[:, head(h)]).astype(BF)

    for i, pair in enumerate(block_loads):
        pair[0].wait()
        pair[1].wait()
        loop(4 * i, 4 * i + 4, kv_sum)
    pl.semaphore_wait(barrier, 19)
    kv.send_core()
    cot_copies[0].start()
    near_cot.start()

    loads[0].wait()
    row = lax.broadcasted_iota(jnp.int32, (256, 256), 0)
    col = lax.broadcasted_iota(jnp.int32, (256, 256), 1)

    def lower(x):
        return jnp.where(row >= col, x, 0.0).astype(BF)

    def upper(x):
        return jnp.where(row <= col, x, 0.0).astype(BF)

    top, low = pl.ds(0, 256), pl.ds(256, 256)

    def causal(a, b, c, h):
        hs = head(h)
        a0, a1, b0, b1, c0, c1 = a[top, hs], a[low, hs], b[top, hs], b[low, hs], c[top, hs], c[low, hs]
        first = nn(lower(nt(a0, b0)), c0)
        second = nn(nt(a1, b0).astype(BF), c0) + nn(lower(nt(a1, b1)), c1)
        return first, second

    def scored(h):
        first, second = causal(q, k, v, h)
        intra[h, top] = first
        intra[h, low] = second

    def turned(h):
        hs = head(h)
        k0, k1, q0, q1 = k[top, hs], k[low, hs], q[top, hs], q[low, hs]
        sup[h, 0] = upper(nt(k0, q0))
        sup[h, 1] = nt(k0, q1).astype(BF)
        sup[h, 2] = upper(nt(k1, q1))

    loop(0, 4, scored)
    kv.send_x()
    cot_copies[1].start()
    cot_copies[2].start()
    loop(4, 16, scored)
    kv.send_up()

    for load in loads[1:4]:
        load.wait()

    def wrows(n):
        return pl.ds(pl.multiple_of(n * 256, 256), 256)

    def grad_own(n):
        gacc[:, wrows(n)] = nt(cot[tp], w[tp, wrows(n), :])

    each(0, 8, grad_own)
    loop(0, 4, turned)
    kv.send_down()
    loop(4, 16, turned)

    def grad_top(n):
        g[top, wrows(n)] = (gacc[top, wrows(n)] + nt(cot[1 - tp, top, :], w[1 - tp, wrows(n), :])).astype(BF)

    def grad_low(n):
        g[low, wrows(n)] = (gacc[low, wrows(n)] + nt(cot[1 - tp, low, :], w[1 - tp, wrows(n), :])).astype(BF)

    loads[4].wait()
    cot_copies[0].wait()
    cot_copies[1].wait()
    each(0, 4, grad_top)
    kv.send_back_x(mem)
    cot_copies[3].start()
    each(4, 8, grad_top)

    def top_rows(h):
        hs = head(h)
        g0 = g[top, hs]
        qacc[h] = tn(q[top, hs], g0)
        gacc[top, hs] = nn(sup[h, 0], g0)
        sup[h, 0] = upper(nt(v[top, hs], g0))

    loop(0, 16, top_rows)
    kv.send_back_core()
    cot_copies[4].start()
    kv.finish()

    def attend(h):
        a = intra[h] + nn(q[:, head(h)], kv.st[h])
        att[0, h // 4, h % 4] = a.T.astype(BF)

    att_copies = []
    for i in range(4):
        loop(4 * i, 4 * i + 4, attend)
        att_copies.append(remote(att.at[0, i], att.at[1, i], at_sem.at[0, i], at_sem.at[1, i], peer_core))
        att_copies[i].start()

    def query_top(h):
        hs = head(h)
        g0 = g[top, hs]
        qg[top, hs] = (nn(lower(nt(g0, v[top, hs])), k[top, hs]) + nt(g0, kv.st[h])).astype(BF)

    def query_low(h):
        hs = head(h)
        g1 = g[low, hs]
        r = nn(nt(g1, v[top, hs]).astype(BF), k[top, hs]) + nn(lower(nt(g1, v[low, hs])), k[low, hs])
        qg[low, hs] = (r + nt(g1, kv.st[h])).astype(BF)

    loop(0, 16, query_top)
    near_cot.wait()
    for copy in att_copies:
        copy.wait()

    y, z = at.y, at.z
    rings = []
    for i in range(4):
        pos, device = (y, at.along_y) if i % 2 == 0 else (z, at.along_z)
        rings.append(Ring(parts[i], lands[i], ring_sem.at[i], pos, device))
    ring_y, ring_z = rings[0], rings[1]
    last_z = Ring(s1a, land_a2, ring_sem.at[4], z, at.along_z)
    last_y = Ring(s1b, land_b2, ring_sem.at[5], y, at.along_y)

    def part(r, i):
        n = rings[r].quarters[i]
        cols = pl.ds(pl.multiple_of(core * 512 + 256 * (r % 2), 256), 256)
        near = cot[tp, :, cols] if r < 2 else cot[1 - tp, :, cols]
        far = pcot[r // 2, :, pl.ds(256 * (r % 2), 256)]
        ours = att[0, :, n] if r % 2 == 0 else att[0, n]
        theirs = att[1, :, n] if r % 2 == 0 else att[1, n]
        total = nn(ours.reshape(512, 512), near) + nn(theirs.reshape(512, 512), far)
        parts[r][n] = total.astype(BF).reshape(2, 2, 128, 256)

    for r in range(2):
        part(r, 2)
        rings[r].send_far()
    for r in range(2):
        for way, i in ((0, 1), (1, 3)):
            part(r, i)
            rings[r].send_near(way)
    for r in range(2):
        part(r, 0)
    for copy in cot_copies[2:]:
        copy.wait()
    far_cot.start()
    each(0, 8, grad_low)
    for r in range(2):
        rings[r].relay(0)
        rings[r].relay(1)

    def qd_sum(h):
        qd.s[h] = (qacc[h] + tn(q[low, head(h)], g[low, head(h)])).astype(BF)

    loop(0, 16, qd_sum)
    qd.send_core()
    far_cot.wait()
    for r in range(2, 4):
        part(r, 2)
        rings[r].send_far()
    part(2, 1)
    rings[2].send_near(0)
    qd.send_x()
    for r, way, i in ((2, 1, 3), (3, 0, 1), (3, 1, 3)):
        part(r, i)
        rings[r].send_near(way)
    for r in range(2, 4):
        part(r, 0)
    loop(0, 8, query_low)
    qd.send_up()
    for r in range(2, 4):
        rings[r].relay(0)
        rings[r].relay(1)
    loop(8, 16, query_low)

    def key_scored(h):
        hs = head(h)
        v0, v1, g1, q1 = v[top, hs], v[low, hs], g[low, hs], q[low, hs]
        intra[h, top] = nn(sup[h, 0], q[top, hs]) + nn(nt(v0, g1).astype(BF), q1)
        intra[h, low] = nn(upper(nt(v1, g1)), q1)

    def value_scored(h):
        g1 = g[low, head(h)]
        gacc[top, head(h)] += nn(sup[h, 1], g1)
        gacc[low, head(h)] = nn(sup[h, 2], g1)

    def stage_two(firsts, second, to):
        for n, first in enumerate(firsts):
            first.wait_results()
            for half in range(2):
                part = first.result(half)
                for i in range(2):
                    to[2 * half + i, :, :, pl.ds(256 * n, 256)] = part[i].astype(BF).reshape(2, 64, 256)
        second.send_far()
        second.send_near(0)
        second.send_near(1)

    loop(0, 4, key_scored)
    qd.send_down()
    stage_two((rings[0], rings[2]), last_z, s1a)
    stage_two((rings[1], rings[3]), last_y, s1b)
    loop(4, 16, key_scored)
    loop(0, 8, value_scored)
    qd.send_back_x(None)
    last_z.relay(0)
    last_z.relay(1)
    last_y.relay(0)
    last_y.relay(1)
    loop(8, 16, value_scored)

    def key_grad(h):
        hs = head(h)
        kg[:, hs] = (intra[h] + nt(v[:, hs], qd.st[h])).astype(BF)

    def value_grad(h):
        hs = head(h)
        vg[:, hs] = (gacc[:, hs] + nn(k[:, hs], qd.st[h])).astype(BF)

    def last(n, i):
        r = (at.p + i) % 4
        return remote(
            fin.at[n, r], fin_land.at[n, at.p], fin_sem.at[0, n, i - 1], fin_sem.at[1, n, i - 1], at.group(r)
        )

    def send_last(n, ring):
        ring.wait_results()
        for half in range(2):
            part = ring.result(half).astype(BF)
            for j in range(2):
                fin[n, half * 2 + j] = part[32 * j : 32 * j + 32]
        for i in range(1, 4):
            last(n, i).start()
        fin_land[n, at.p] = fin[n, at.p]

    send_last(0, last_z)
    send_last(1, last_y)
    qd.send_back_core()
    loop(0, 8, lambda i: key_grad(8 * core + i))
    loop(0, 8, lambda i: value_grad(8 * core + i))
    qd.finish()
    loop(0, 8, lambda i: key_grad(8 * (1 - core) + i))
    loop(0, 8, lambda i: value_grad(8 * (1 - core) + i))
    for n in range(2):
        for i in range(1, 4):
            last(n, i).wait()
    for c in range(2):
        for n in range(2):
            total = fin_land[n, c].astype(F32) + fin_land[n, 2 + c].astype(F32)
            for i in range(2):
                start = (tp if i == 0 else 1 - tp) * 1024 + c * 512 + 256 * n
                wg[:, pl.ds(pl.multiple_of(start, 256), 256)] = total[:, 256 * i : 256 * i + 256]


def scan_scratch(kind):
    piece = VM((16, 32, 128), kind)
    return (
        VM((16, 128, 128), BF),
        VM((8, 128, 128), BF),
        VM((2, 4, 128, 128), BF),
        VM((4, 128, 128), BF),
        piece, piece, piece, piece,
        VM((4, 128, 128), F32),
        VM((4, 128, 128), BF),
        VM((4, 128, 128), BF),
        VM((8, 128, 128), BF),
        VM((16, 128, 128), BF),
        DMA((2, 4)),
        DMA((2,)),
        DMA((2,)),
    )


def put_out(*refs):
    sems = refs[8]
    copies = [pltpu.make_async_copy(refs[3], refs[7], sems.at[0])]
    for i in range(3):
        for j in range(4):
            rows = pl.ds(128 * j, 128)
            copies.append(pltpu.make_async_copy(refs[i].at[rows], refs[4 + i].at[rows], sems.at[1 + 4 * i + j]))
    for copy in copies:
        copy.start()
    for copy in copies:
        copy.wait()


def local(queries, keys, values, cotangent, out_weight, memory):
    tok = VM((512, 2048), BF)
    any_spec = pl.BlockSpec(memory_space=pl.ANY)
    like = jax.ShapeDtypeStruct((512, 2048), BF)
    grads = pl.pallas_call(
        kernel,
        out_shape=(VM((512, 2048), BF), VM((512, 2048), BF), VM((512, 2048), BF), VM((32, 2048), F32)),
        in_specs=[any_spec] * 6,
        out_specs=(pl.BlockSpec(memory_space=VM),) * 4,
        scratch_shapes=[
            tok, tok, tok,
            VM((2, 2048, 1024), BF),
            VM((2, 512, 1024), BF),
            VM((2, 512, 512), BF),
            VM((4, 128, 128), F32),
            VM((512, 2048), F32),
            tok,
            VM((16, 512, 128), F32),
            scan_scratch(F32),
            scan_scratch(BF),
            VM((16, 3, 256, 256), BF),
            VM((16, 128, 128), F32),
            VM((2, 4, 4, 128, 512), BF),
            (VM((4, 2, 2, 128, 256), BF),) * 4,
            (VM((2, 3, 2, 128, 256), BF),) * 4,
            VM((4, 2, 64, 512), BF),
            VM((4, 2, 64, 512), BF),
            VM((2, 3, 64, 512), BF),
            VM((2, 3, 64, 512), BF),
            VM((2, 4, 32, 512), BF),
            VM((2, 4, 32, 512), BF),
            DMA((15,)),
            DMA((2, 5)),
            DMA((2, 2)),
            DMA((2, 4)),
            DMA((6, 2, 2, 3)),
            DMA((2, 2, 3)),
        ],
        compiler_params=pltpu.CompilerParams(
            collective_id=0, has_side_effects=True, vmem_limit_bytes=59768832
        ),
    )(queries, keys, values, cotangent, out_weight, memory)
    return pl.pallas_call(
        put_out,
        out_shape=(like, like, like, jax.ShapeDtypeStruct((32, 2048), F32)),
        in_specs=[any_spec] * 4,
        out_specs=(any_spec,) * 4,
        scratch_shapes=[DMA((13,))],
        compiler_params=pltpu.CompilerParams(vmem_limit_bytes=1048576),
    )(*grads)


def solution(mesh):
    in_specs = (
        P("ctx", "tp"),
        P("ctx", "tp"),
        P("ctx", "tp"),
        P("ctx", "tp"),
        P("tp", None),
        P("tp", None, None),
    )
    out_specs = (P("ctx", "tp"), P("ctx", "tp"), P("ctx", "tp"), P(("tp", "ctx"), None))
    return jax.shard_map(local, mesh=mesh, in_specs=in_specs, out_specs=out_specs, check_vma=False)
```
